32 devices in a mesh: groups: 2 (over y), fsdp: 4 (over x, core), tensor: 4 (over z).
Axes of the slice: x: 2, y: 2, z: 4, core: 2. Of those that a mesh axis runs over, the one named last changes fastest.
Arguments:
- tokens: bfloat16 [1024, 8192], P(('groups', 'fsdp')), parts along dimension 0, may hold values from -64 to 64
- gate_weight: bfloat16 [8192, 14336], P('fsdp', 'tensor'), may hold values from -0.0625 to 0.0625
- up_weight: bfloat16 [8192, 14336], P('fsdp', 'tensor'), may hold values from -0.0625 to 0.0625
- down_weight: bfloat16 [14336, 8192], P('tensor', 'fsdp'), may hold values from -0.046875 to 0.046875
- right_factor: bfloat16 [64, 128, 128], P('fsdp', 'tensor'), may hold values from -0.5 to 0.5
- left_factor: bfloat16 [128, 64, 64], P('fsdp', 'tensor'), may hold values from -0.75 to 0.75
Outputs:
- grad_right: float32 [128, 128, 128], P(('groups', 'fsdp'), 'tensor'), parts along dimension 0
- grad_left: float32 [256, 64, 64], P(('groups', 'fsdp'), 'tensor'), parts along dimension 0
The draws below stay inside these ranges and needn't reach their ends.
There are 2 independent parts, one for each index of `groups`. The reference program is written for one: setup_inputs(seed, part) draws one part's arguments, and reference() takes and returns one part's arrays. A program takes and returns all parts, laid end to end along the dimension named above; an argument that names none is the same for every part. Nothing has to cross between parts.
All inputs are finite; a program needn't handle non-finite values.
Results may differ from the reference program's by a relative error of at most 0.0055.
Values may be sent and summed in bfloat16 or wider, within the bound.
A program may use at most 128 MiB of HBM per device.

```python
import math
import jax
import jax.numpy as jnp
from jax import lax

D = 8192
FF = 14336
NBLK = 64
BSZ = 128
TOKENS = 512
FEAT_SHARE = 2048
HIDDEN_SHARE = 3584


def draw_tokens(key, part):
    base_key, row_key, col_key = jax.random.split(jax.random.fold_in(key, 11), 3)
    base = jnp.clip(jax.random.normal(base_key, (TOKENS, D), jnp.float32), -6.0, 6.0)
    row_scale = jnp.exp(jax.random.uniform(row_key, (TOKENS, 1), jnp.float32, -0.1, 0.1))
    col_scale = 0.6 * jnp.exp(jax.random.uniform(col_key, (1, D), jnp.float32, -1.15, 1.15))
    return (base * row_scale * col_scale).astype(jnp.bfloat16)


def levels(stream_key, shape, pieces, smallest, top_value):
    loudness, own = 1.0, jax.random.fold_in(stream_key, 6)
    for position, blocks in pieces:
        draws = jnp.exp(jax.random.uniform(jax.random.fold_in(own, position), (blocks,), jnp.float32, smallest / len(pieces), top_value / len(pieces)))
        loudness = loudness * jnp.repeat(draws, shape[position] // blocks).reshape([-1 if axis == position else 1 for axis in range(len(shape))])
    return loudness


def centred(own_key, extent, spread, limit, cuts=(), dtype=jnp.bfloat16):
    factor_of = levels(own_key, extent, cuts, -0.22, 0.18) if cuts else 1.0
    array = jax.random.normal(own_key, extent, jnp.float32) * spread * factor_of
    return jnp.minimum(jnp.maximum(array, -limit), limit).astype(dtype)


def setup_inputs(seed: int = 0, part: int = 0) -> dict:
    splits = jax.random.split(jax.random.key(seed), 7)
    part_keys = jax.random.split(jax.random.fold_in(splits[6], part), 7)
    tokens = draw_tokens(jax.random.fold_in(jax.random.fold_in(splits[6], part), 71), part)
    gate_weight = centred(splits[1], (D, FF), D ** -0.5, 0.0625, ((0, 4), (1, 4)))
    up_weight = centred(splits[2], (D, FF), D ** -0.5, 0.0625, ((0, 4), (1, 4)))
    down_weight = centred(splits[3], (FF, D), FF ** -0.5, 0.046875, ((0, 4), (1, 4)))
    right_factor = centred(splits[4], (NBLK, BSZ, BSZ), BSZ ** -0.5, 0.5, ((0, 4), (1, 4)))
    left_factor = centred(splits[5], (BSZ, NBLK, NBLK), NBLK ** -0.5, 0.75, ((0, 4), (1, 4)))
    return dict(tokens=tokens, gate_weight=gate_weight, up_weight=up_weight, down_weight=down_weight, right_factor=right_factor, left_factor=left_factor)


def grouped_product(left_parts, right_parts, rows, width):

    def add_group(total, pair):
        product = jnp.dot(pair[0], pair[1], preferred_element_type=jnp.float32)
        rounded = lax.optimization_barrier(product.astype(jnp.bfloat16))
        return (total + rounded.astype(jnp.float32), None)
    start = jnp.zeros((rows, width), jnp.float32)
    return lax.scan(add_group, start, (left_parts, right_parts))[0]

def reference(tokens, gate_weight, up_weight, down_weight, right_factor, left_factor):
    feature_groups = D // FEAT_SHARE
    hidden_groups = FF // HIDDEN_SHARE
    token_parts = jnp.moveaxis(tokens.reshape(TOKENS, feature_groups, FEAT_SHARE), 1, 0)
    gate_sum = grouped_product(token_parts, gate_weight.reshape(feature_groups, FEAT_SHARE, FF), TOKENS, FF)
    up_sum = grouped_product(token_parts, up_weight.reshape(feature_groups, FEAT_SHARE, FF), TOKENS, FF)
    hidden = (jax.nn.silu(gate_sum) * up_sum).astype(jnp.bfloat16)
    hidden_parts = jnp.moveaxis(hidden.reshape(TOKENS, hidden_groups, HIDDEN_SHARE), 1, 0)
    target = grouped_product(hidden_parts, down_weight.reshape(hidden_groups, HIDDEN_SHARE, D), TOKENS, D)
    block_input = tokens.reshape(TOKENS, NBLK, BSZ).astype(jnp.float32)
    mixed = jnp.einsum('nij,ikj->nik', block_input, right_factor.astype(jnp.float32)).astype(jnp.bfloat16)
    left_wide = left_factor.astype(jnp.float32)
    mixed_wide = mixed.astype(jnp.float32)
    student = jnp.einsum('nij,jki->njk', mixed_wide, left_wide)
    out_grad = (student - target.reshape(TOKENS, BSZ, NBLK)) / math.sqrt(TOKENS)
    grad_left = jnp.einsum('njk,nij->jki', out_grad, mixed_wide)
    mixed_grad = jnp.einsum('njk,jki->nij', out_grad, left_wide).astype(jnp.bfloat16)
    grad_right = jnp.einsum('nik,nij->ikj', mixed_grad.astype(jnp.float32), block_input)
    return (grad_right, grad_left)
```

```python
import functools
import math

import jax
import jax.numpy as jnp
from jax import lax
from jax.experimental import pallas as pl
from jax.experimental.pallas import tpu as pltpu
from jax.sharding import PartitionSpec as P

MESH = pl.DeviceIdType.MESH
CHUNK = 512
SUB = 16
GROUPS = ((0, 2), (2, 4), (4, 6), (6, 8))


def plain_body(tokens, gate_weight, up_weight, down_weight, right_factor, left_factor):
    fsdp_count = lax.axis_size("fsdp")
    tensor_count = lax.axis_size("tensor")
    tok_local = tokens.shape[0]
    group_rows = tok_local * fsdp_count
    share_rows = group_rows // tensor_count
    hid_local = gate_weight.shape[1]
    spread = lax.all_to_all(tokens, "fsdp", split_axis=1, concat_axis=0, tiled=True)
    student_in = lax.dynamic_slice_in_dim(
        spread, lax.axis_index("tensor") * share_rows, share_rows, 0
    )
    gate_part = jnp.dot(spread, gate_weight, preferred_element_type=jnp.float32)
    up_part = jnp.dot(spread, up_weight, preferred_element_type=jnp.float32)
    partial_value = jnp.concatenate([gate_part, up_part], axis=1)
    summed = lax.psum(partial_value.astype(jnp.bfloat16), "fsdp").astype(jnp.float32)
    hidden = (jax.nn.silu(summed[:, :hid_local]) * summed[:, hid_local:]).astype(jnp.bfloat16)
    target = lax.psum_scatter(
        jnp.dot(hidden, down_weight, preferred_element_type=jnp.float32).astype(jnp.bfloat16),
        "tensor",
        scatter_dimension=0,
        tiled=True,
    ).astype(jnp.float32)
    right_full, left_full = (
        lax.all_gather(right_factor, "tensor", axis=1, tiled=True),
        lax.all_gather(left_factor, "tensor", axis=1, tiled=True),
    )
    blocks_local = right_full.shape[0]
    block_size = right_full.shape[2]
    block_input = student_in.reshape(share_rows, blocks_local, block_size)
    mixed = jnp.einsum(
        "nij,ikj->nik", block_input, right_full, preferred_element_type=jnp.float32
    ).astype(jnp.bfloat16)
    routed = lax.all_to_all(mixed, "fsdp", split_axis=2, concat_axis=1, tiled=True)
    student = jnp.einsum("nij,jki->njk", routed, left_full, preferred_element_type=jnp.float32)
    inv_root = 1.0 / math.sqrt(group_rows)
    out_grad = (student - target.reshape(student.shape)) * inv_root
    grad_left = jnp.einsum("njk,nij->jki", out_grad, routed.astype(jnp.float32))
    mixed_grad = jnp.einsum("njk,jki->nij", out_grad, left_full.astype(jnp.float32)).astype(
        jnp.bfloat16
    )
    returned = lax.all_to_all(mixed_grad, "fsdp", split_axis=1, concat_axis=2, tiled=True)
    grad_right = jnp.einsum(
        "nik,nij->ikj", returned.astype(jnp.float32), block_input.astype(jnp.float32)
    )
    grad_right, grad_left = (
        lax.psum_scatter(grad_right, "tensor", scatter_dimension=1, tiled=True),
        lax.psum_scatter(grad_left, "tensor", scatter_dimension=1, tiled=True),
    )
    return (grad_right, grad_left)


def layer_kernel(
    n, T, width, cols,
    tok, gw, uw, dw, right, left, gr_out, gl_out,
    wg, wu, wd, pbuf, recv_p, recv_x, hid, t_send, t_recv,
    spread, rload, r_s, rki, lji, rbig, lbig, mix_s, routed, mg_s, mg_r, gr_s, gl_acc, gl_s,
    tok_send, tok_recv, tx_send, tx_recv, tf_send, tf_recv, w_sem, d_sem,
    p_send, p_recv, a_send, a_recv, hx_send, hx_recv, hp_send, hp_recv, r_send, r_recv,
    z_send, z_recv, rf_send, rf_recv, lf_send, lf_recv, mix_send, mix_recv, mg_send, mg_recv,
    gr_send, gr_recv, gl_send, gl_recv,
):
    f32, bf16 = jnp.float32, jnp.bfloat16
    f = lax.axis_index("fsdp")
    z = lax.axis_index("tensor")
    x, c = f // 2, f % 2
    partner = x * 2 + (1 - c)
    across = (1 - x) * 2 + c
    diag = (1 - x) * 2 + (1 - c)
    peers = (across, diag, partner)
    parts, rows, features = spread.shape[0], spread.shape[2], spread.shape[3]
    N = parts * 4 * rows
    G = len(GROUPS)
    ni, nk_local, nj = right.shape
    na = nk_local // T
    nk, nb = left.shape[1] * T, left.shape[2]
    nf = na * ni
    iota = functools.partial(lax.broadcasted_iota, jnp.int32)

    def to(peer):
        return dict(device_id={"fsdp": peer}, device_id_type=MESH)

    def along(peer):
        return dict(device_id={"tensor": peer}, device_id_type=MESH)

    def tile(t):
        return pl.ds(pl.multiple_of(t * width, width), width)

    def token_rows(g):
        return slice(GROUPS[g][0] * 4 * rows, GROUPS[g][1] * 4 * rows)

    def weights(t):
        s = lax.rem(t, 2)
        cc = tile(lax.rem(t, n))
        return (
            pltpu.make_async_copy(gw.at[:, cc], wg.at[s], w_sem.at[0, s]),
            pltpu.make_async_copy(uw.at[:, cc], wu.at[s], w_sem.at[1, s]),
        )

    def feature_columns(peer):
        return pl.ds(pl.multiple_of(peer * features, features), features)

    own = pltpu.make_async_copy(
        tok.at[:, :, feature_columns(f)], spread.at[:, f], tok_send.at[0])
    own.start()
    for cp in weights(0):
        cp.start()
    load_right = pltpu.make_async_copy(right, rload, rf_send.at[0])
    load_right.start()

    barrier = pltpu.get_barrier_semaphore()
    for peer in peers:
        pl.semaphore_signal(barrier, inc=1, **to(peer))
    for d in range(1, T):
        pl.semaphore_signal(barrier, inc=1, **along(lax.rem(z + d, T)))
    pl.semaphore_wait(barrier, 3 + T - 1)

    half = lax.rem(z, 2)
    z_mate = z + 1 - 2 * half
    span = parts // 4

    def tok_cross(i, j):
        mm = pl.ds(half * (parts // 2) + j * span, span)
        return pltpu.make_async_remote_copy(
            tok.at[mm, :, feature_columns(peers[i])], spread.at[mm, f],
            tx_send.at[i, j], tx_recv.at[i, j], **to(peers[i]))

    def tok_pass(i, j):
        mm = pl.ds(half * (parts // 2) + j * span, span)
        return pltpu.make_async_remote_copy(
            spread.at[mm, peers[i]], spread.at[mm, peers[i]],
            tf_send.at[i, j], tf_recv.at[i, j], **along(z_mate))

    tok_near = pltpu.make_async_remote_copy(
        tok.at[:, :, feature_columns(partner)], spread.at[:, f],
        tok_send.at[1], tok_recv.at[1], **to(partner))
    tok_near.start()
    pieces = [(i, j) for j in range(2) for i in range(2)]
    for i, j in pieces:
        tok_cross(i, j).start()

    load_right.wait()
    wide_right = rload[...].astype(f32)
    for p in range(T):
        r_s[p] = wide_right[:, p * na:(p + 1) * na].reshape(nf, nj).astype(bf16)

    def right_copy(d):
        peer = lax.rem(z + d, T)
        return pltpu.make_async_remote_copy(
            r_s.at[peer], rki.at[z], rf_send.at[d], rf_recv.at[d], **along(peer))

    def left_copy(d):
        peer = lax.rem(z + d, T)
        return pltpu.make_async_remote_copy(
            left.at[pl.ds(peer * na, na)], lji.at[:, z], lf_send.at[d], lf_recv.at[d],
            **along(peer))

    factors = [right_copy(d) for d in range(1, T)] + [left_copy(d) for d in range(1, T)]
    for cp in factors:
        cp.start()
    own_left = pltpu.make_async_copy(left.at[pl.ds(z * na, na)], lji.at[:, z], lf_send.at[0])
    own_left.start()
    rki[z] = r_s[z]

    def pair_copy(p, t):
        cc = tile(t)
        return pltpu.make_async_remote_copy(
            pbuf.at[p, 1 - c, :, :, :, cc], recv_p.at[p, :, :, :, cc],
            p_send.at[p, t], p_recv.at[p, t], **to(partner))

    def pair_sum(p, t):
        pair_copy(p, t).wait_recv()
        cc = tile(t)
        for k in range(2):
            total = pbuf[p, c, :, k, :, cc].astype(f32) + recv_p[p, :, k, :, cc].astype(f32)
            pbuf[p, c, :, k, :, cc] = total.astype(bf16)

    def products(p, t):
        chip = x if p == 0 else 1 - x
        step = p * n + t

        @pl.when(step + 1 < 2 * n)
        def _():
            for cp in weights(step + 1):
                cp.start()

        for cp in weights(step):
            cp.wait()
        s = lax.rem(step, 2)
        toks = spread[:, pl.ds(2 * chip, 2)].reshape(parts * 2 * rows, features)
        cc = tile(t)
        for k, w in ((0, wg), (1, wu)):
            part = jnp.dot(toks, w[s], preferred_element_type=f32).astype(bf16)
            part = part.reshape(parts, 2, rows, width)
            for h in range(2):
                pbuf[p, h, :, k, :, cc] = part[:, h]
        pair_copy(p, t).start()

        @pl.when(t >= 1)
        def _():
            pair_sum(p, t - 1)

    own.wait()
    tok_near.wait_recv()

    def first_half(t, carry):
        products(0, t)
        for q, (i, j) in enumerate(pieces):
            @pl.when(t == 2 * q + 1)
            def _():
                tok_cross(i, j).wait_recv()
                tok_pass(i, j).start()
        return carry

    lax.fori_loop(0, n, first_half, 0)
    pair_sum(0, n - 1)

    def send_a(g):
        mm = slice(*GROUPS[g])
        return pltpu.make_async_remote_copy(
            pbuf.at[0, c, mm], recv_x.at[mm], a_send.at[g], a_recv.at[g], **to(across))

    send_a(0).start()
    for q, (i, j) in enumerate(pieces):
        if 2 * q + 1 >= n:
            tok_cross(i, j).wait_recv()
            tok_pass(i, j).start()

    own_left.wait()
    for cp in factors:
        cp.wait()
    packed = rki[...].reshape(T * nf, nj)
    lane_block = lax.rem(iota((T * nf, nj), 0), nf) // na
    for i in range(ni):
        rbig[:, i * nj:(i + 1) * nj] = jnp.where(lane_block == i, packed, jnp.zeros_like(packed))
    col = lax.rem(iota((nb, 4 * nf), 1), nf)
    pick = iota((nb, 4 * nf), 0) == (iota((nb, 4 * nf), 1) // nf) * ni + col // na
    wide = jnp.dot(
        lji[...].reshape(na * nk, nb), pick.astype(f32).astype(bf16), preferred_element_type=f32)
    same = iota((na * nk, 4 * nf), 0) // nk == lax.rem(iota((na * nk, 4 * nf), 1), na)
    lbig[...] = jnp.where(same, wide, 0.0).astype(bf16)

    for i, j in pieces:
        tok_pass(i, j).wait_recv()

    def second_half(t, carry):
        products(1, t)
        return carry

    lax.fori_loop(0, n, second_half, 0)
    load_down = pltpu.make_async_copy(dw, wd, d_sem)
    load_down.start()
    pair_sum(1, n - 1)

    def mix_copy(i):
        return pltpu.make_async_remote_copy(
            mix_s.at[:, pl.ds(pl.multiple_of(peers[i] * nf, nf), nf)],
            routed.at[:, pl.ds(pl.multiple_of(f * nf, nf), nf)],
            mix_send.at[i], mix_recv.at[i], **to(peers[i]))

    mix_s[...] = lax.dot_general(
        spread[...].reshape(N, features), rbig[...], (((1,), (1,)), ((), ())),
        preferred_element_type=f32).astype(bf16)
    for i in range(3):
        mix_copy(i).start()
    mine = pl.ds(pl.multiple_of(f * nf, nf), nf)
    routed[:, mine] = mix_s[:, mine]
    send_a(1).start()

    def send_hx(g):
        mm = slice(*GROUPS[g])
        return pltpu.make_async_remote_copy(
            hid.at[mm, across], hid.at[mm, across], hx_send.at[g], hx_recv.at[g], **to(across))

    def send_hp(g):
        mm = slice(*GROUPS[g])
        return pltpu.make_async_remote_copy(
            hid.at[mm, across], hid.at[mm, across], hp_send.at[g], hp_recv.at[g], **to(partner))

    def send_r(g):
        mm = slice(*GROUPS[g])
        return pltpu.make_async_remote_copy(
            hid.at[mm, f], hid.at[mm, f], r_send.at[g], r_recv.at[g], **to(partner))

    def z_copy(g, d):
        rr = token_rows(g)
        peer = lax.rem(z + d, T)
        return pltpu.make_async_remote_copy(
            t_send.at[peer, rr], t_recv.at[d - 1, rr], z_send.at[g, d], z_recv.at[g, d],
            **along(peer))

    def mg_copy(g, i):
        rr = token_rows(g)
        return pltpu.make_async_remote_copy(
            mg_s.at[rr, pl.ds(pl.multiple_of(peers[i] * nf, nf), nf)], mg_r.at[f, rr],
            mg_send.at[g, i], mg_recv.at[g, i], **to(peers[i]))

    def make_hidden(g):
        mm = slice(*GROUPS[g])
        send_a(g).wait_recv()

        @pl.loop(0, n)
        def _(t):
            cc = tile(t)
            gate = pbuf[1, c, mm, 0, :, cc].astype(f32) + recv_x[mm, 0, :, cc].astype(f32)
            up = pbuf[1, c, mm, 1, :, cc].astype(f32) + recv_x[mm, 1, :, cc].astype(f32)
            hid[mm, across, :, cc] = (jax.nn.silu(gate) * up).astype(bf16)

        send_hx(g).start()
        send_hp(g).start()

    def make_target(g):
        m0, m1 = GROUPS[g]
        rr = token_rows(g)
        send_hx(g).wait_recv()
        send_r(g).start()
        send_hp(g).wait_recv()
        send_r(g).wait_recv()

        @pl.loop(0, T)
        def _(i):
            b = lax.rem(z + 1 + i, T)
            cc = pl.ds(pl.multiple_of(b * cols, cols), cols)
            h = hid[m0:m1].reshape((m1 - m0) * 4 * rows, n * width)
            t_send[b, rr] = jnp.dot(h, wd[:, cc], preferred_element_type=f32).astype(bf16)

            @pl.when(i < T - 1)
            def _():
                z_copy(g, i + 1).start()

    def make_grads(g, first):
        rr = token_rows(g)
        student = lax.dot_general(
            routed[rr], lbig[...], (((1,), (1,)), ((), ())), preferred_element_type=f32)
        tgt = t_send[z, rr].astype(f32)
        for d in range(1, T):
            z_copy(g, d).wait_recv()
            tgt = tgt + t_recv[d - 1, rr].astype(f32)
        out_grad = (student - tgt) * (1.0 / math.sqrt(N))
        mg_s[rr] = jnp.dot(
            out_grad.astype(bf16), lbig[...], preferred_element_type=f32).astype(bf16)
        for i in range(3):
            mg_copy(g, i).start()
        mg_r[f, rr] = mg_s[rr, mine]
        part = jnp.dot(out_grad.T.astype(bf16), routed[rr], preferred_element_type=f32)
        if first:
            gl_acc[...] = part
        else:
            gl_acc[...] += part

    row_block = iota((nf, nj), 0) // na

    def right_terms(b, m0, m1):
        rr = slice(m0 * 4 * rows, m1 * 4 * rows)
        flipped = mg_r[b, rr].astype(f32).T.astype(bf16)
        total = jnp.zeros((nf, nj), f32)
        for i in range(0, ni, 2):
            rhs = spread[m0:m1, :, :, i * nj:(i + 2) * nj].reshape((m1 - m0) * 4 * rows, 2 * nj)
            part = jnp.dot(flipped, rhs, preferred_element_type=f32)
            for k in range(2):
                total += jnp.where(row_block == i + k, part[:, k * nj:(k + 1) * nj], 0.0)
        return total.reshape(ni, na, nj)

    for g in range(G):
        make_hidden(g)
        if g + 2 < G:
            send_a(g + 2).start()
        if g == 0:
            for i in range(3):
                mix_copy(i).wait_recv()
        if g == 1:
            load_down.wait()
        if g >= 2:
            make_grads(g - 2, g == 2)
        if g >= 1:
            make_target(g - 1)
    make_grads(G - 2, G == 2)
    make_target(G - 1)

    early = GROUPS[G - 1][0]
    for g in range(G - 1):
        for i in range(3):
            mg_copy(g, i).wait_recv()

    @pl.loop(0, 4)
    def _(b):
        gr_s[b] = right_terms(b, 0, early)

    def gl_copy(d):
        peer = lax.rem(z + d, T)
        return pltpu.make_async_remote_copy(
            gl_s.at[:, peer], gl_out.at[pl.ds(z * na, na)], gl_send.at[d], gl_recv.at[d],
            **along(peer))

    def gr_copy(b):
        return pltpu.make_async_remote_copy(
            gr_s.at[b], gr_out.at[:, pl.ds(pl.multiple_of(z * na, na), na)],
            gr_send.at[b], gr_recv.at[z], **along(b))

    make_grads(G - 1, False)

    keep = iota((na * nk, nf), 0) // nk == lax.rem(iota((na * nk, nf), 1), na)
    total = jnp.zeros((na * nk, nb), f32)
    for b in range(4):
        fold = iota((nf, nb), 1) == b * ni + iota((nf, nb), 0) // na
        total += jnp.dot(
            jnp.where(keep, gl_acc[:, b * nf:(b + 1) * nf], 0.0), fold.astype(f32),
            precision=lax.Precision.HIGHEST, preferred_element_type=f32)
    gl_s[...] = total.reshape(na, T, nk // T, nb)
    for d in range(1, T):
        gl_copy(d).start()
    gl_out[pl.ds(z * na, na)] = gl_s[:, z]

    def finish_right(b):
        gr_s[b] += right_terms(b, early, parts)

        @pl.when(b != z)
        def _():
            gr_copy(b).start()

        @pl.when(b == z)
        def _():
            gr_out[:, pl.ds(pl.multiple_of(z * na, na), na)] = gr_s[b]

    finish_right(f)
    for i in (2, 0, 1):
        mg_copy(G - 1, i).wait_recv()
        finish_right(peers[i])

    for d in range(1, T):
        gl_copy(d).wait()
    for b in range(T):
        @pl.when(z != b)
        def _():
            gr_copy(b).wait_send()
            pltpu.make_async_remote_copy(
                gr_s.at[b], gr_out.at[:, pl.ds(pl.multiple_of(z * na, na), na)],
                gr_send.at[b], gr_recv.at[b], **along(b)).wait_recv()

    tok_near.wait_send()
    for i, j in pieces:
        tok_cross(i, j).wait_send()
        tok_pass(i, j).wait_send()
    for i in range(3):
        mix_copy(i).wait_send()
    for g in range(G):
        for cp in (send_a(g), send_hx(g), send_hp(g), send_r(g)):
            cp.wait_send()
        for d in range(1, T):
            z_copy(g, d).wait_send()
        for i in range(3):
            mg_copy(g, i).wait_send()

    def drain(t, carry):
        for p in range(2):
            pair_copy(p, t).wait_send()
        return carry

    lax.fori_loop(0, n, drain, 0)


def fused_body(tokens, gate_weight, up_weight, down_weight, right_factor, left_factor):
    T = lax.axis_size("tensor")
    rows = SUB
    parts = tokens.shape[0] // rows
    tok = tokens.reshape(parts, rows, tokens.shape[1])
    features, hidden = gate_weight.shape
    width = CHUNK
    n = hidden // width
    G = len(GROUPS)
    cols = down_weight.shape[1] // T
    bf16, f32 = jnp.bfloat16, jnp.float32
    dma = pltpu.SemaphoreType.DMA
    anyspace = pl.BlockSpec(memory_space=pl.ANY)
    vmem = pl.BlockSpec(memory_space=pltpu.VMEM)
    ni, nkr, nj = right_factor.shape
    na, nkl, nb = left_factor.shape[0] // T, left_factor.shape[1], left_factor.shape[2]
    nf, nk = na * ni, nkl * T
    N = 4 * parts * rows
    return pl.pallas_call(
        functools.partial(layer_kernel, n, T, width, cols),
        out_shape=(
            jax.ShapeDtypeStruct((ni, nkr, nj), f32),
            jax.ShapeDtypeStruct((T * na, nkl, nb), f32),
        ),
        in_specs=[anyspace] * 6,
        out_specs=(vmem, vmem),
        scratch_shapes=[
            pltpu.VMEM((2, features, width), bf16),
            pltpu.VMEM((2, features, width), bf16),
            pltpu.VMEM((hidden, T * cols), bf16),
            pltpu.VMEM((2, 2, parts, 2, rows, hidden), bf16),
            pltpu.VMEM((2, parts, 2, rows, hidden), bf16),
            pltpu.VMEM((parts, 2, rows, hidden), bf16),
            pltpu.VMEM((parts, 4, rows, hidden), bf16),
            pltpu.VMEM((T, N, cols), bf16),
            pltpu.VMEM((T - 1, N, cols), bf16),
            pltpu.VMEM((parts, 4, rows, features), bf16),
            pltpu.VMEM((ni, nkr, nj), bf16),
            pltpu.VMEM((T, nf, nj), bf16),
            pltpu.VMEM((T, nf, nj), bf16),
            pltpu.VMEM((na, T, nkl, nb), bf16),
            pltpu.VMEM((4 * nf, features), bf16),
            pltpu.VMEM((na * nk, 4 * nf), bf16),
            pltpu.VMEM((N, 4 * nf), bf16),
            pltpu.VMEM((N, 4 * nf), bf16),
            pltpu.VMEM((N, 4 * nf), bf16),
            pltpu.VMEM((4, N, nf), bf16),
            pltpu.VMEM((4, ni, na, nj), f32),
            pltpu.VMEM((na * nk, 4 * nf), f32),
            pltpu.VMEM((na, T, nkl, nb), f32),
            dma((2,)), dma((2,)), dma((2, 2)), dma((2, 2)), dma((2, 2)), dma((2, 2)),
            dma((2, 2)), dma,
            dma((2, n)), dma((2, n)), dma((G,)), dma((G,)),
            dma((G,)), dma((G,)), dma((G,)), dma((G,)), dma((G,)), dma((G,)),
            dma((G, T)), dma((G, T)),
            dma((T,)), dma((T,)), dma((T,)), dma((T,)),
            dma((3,)), dma((3,)), dma((G, 3)), dma((G, 3)),
            dma((T,)), dma((T,)), dma((T,)), dma((T,)),
        ],
        compiler_params=pltpu.CompilerParams(
            collective_id=0, has_side_effects=True, vmem_limit_bytes=62 * 1024 * 1024
        ),
        name="layer",
    )(tok, gate_weight, up_weight, down_weight, right_factor, left_factor)


def body(tokens, gate_weight, up_weight, down_weight, right_factor, left_factor):
    F, T = lax.axis_size("fsdp"), lax.axis_size("tensor")
    fits = (
        F == 4
        and T == 4
        and gate_weight.shape[1] % CHUNK == 0
        and left_factor.shape[0] % T == 0
        and right_factor.shape[1] % T == 0
        and gate_weight.shape[0] <= 2048
        and tokens.shape[0] == 128
    )
    run = fused_body if fits else plain_body
    return run(tokens, gate_weight, up_weight, down_weight, right_factor, left_factor)


def solution(mesh):
    return jax.shard_map(
        body,
        mesh=mesh,
        in_specs=(
            P(("groups", "fsdp"), None),
            P("fsdp", "tensor"),
            P("fsdp", "tensor"),
            P("tensor", "fsdp"),
            P("fsdp", "tensor", None),
            P("fsdp", "tensor", None),
        ),
        out_specs=(P(("groups", "fsdp"), "tensor", None), P(("groups", "fsdp"), "tensor", None)),
        check_vma=False,
    )
```

```python
import functools
import math

import jax
import jax.numpy as jnp
from jax import lax
from jax.experimental import pallas as pl
from jax.experimental.pallas import tpu as pltpu
from jax.sharding import PartitionSpec as P

MESH = pl.DeviceIdType.MESH
CHUNK = 512
SUB = 16
GROUPS = ((0, 2), (2, 4), (4, 6), (6, 7), (7, 8))
DEPTH = 3
LATE = 3
PLAN = (
    "h0 h1 a2 m d t0 t1 c0 c1 "
    "h2 a3 a4 w g0 g1 t2 "
    "h3 c2 h4 g2 t3 t4 "
    "c3 c4 r g3 g4"
)


def plain_body(tokens, gate_weight, up_weight, down_weight, right_factor, left_factor):
    fsdp_count = lax.axis_size("fsdp")
    tensor_count = lax.axis_size("tensor")
    tok_local = tokens.shape[0]
    group_rows = tok_local * fsdp_count
    share_rows = group_rows // tensor_count
    hid_local = gate_weight.shape[1]
    spread = lax.all_to_all(tokens, "fsdp", split_axis=1, concat_axis=0, tiled=True)
    student_in = lax.dynamic_slice_in_dim(
        spread, lax.axis_index("tensor") * share_rows, share_rows, 0
    )
    gate_part = jnp.dot(spread, gate_weight, preferred_element_type=jnp.float32)
    up_part = jnp.dot(spread, up_weight, preferred_element_type=jnp.float32)
    partial_value = jnp.concatenate([gate_part, up_part], axis=1)
    summed = lax.psum(partial_value.astype(jnp.bfloat16), "fsdp").astype(jnp.float32)
    hidden = (jax.nn.silu(summed[:, :hid_local]) * summed[:, hid_local:]).astype(jnp.bfloat16)
    target = lax.psum_scatter(
        jnp.dot(hidden, down_weight, preferred_element_type=jnp.float32).astype(jnp.bfloat16),
        "tensor",
        scatter_dimension=0,
        tiled=True,
    ).astype(jnp.float32)
    right_full, left_full = (
        lax.all_gather(right_factor, "tensor", axis=1, tiled=True),
        lax.all_gather(left_factor, "tensor", axis=1, tiled=True),
    )
    blocks_local = right_full.shape[0]
    block_size = right_full.shape[2]
    block_input = student_in.reshape(share_rows, blocks_local, block_size)
    mixed = jnp.einsum(
        "nij,ikj->nik", block_input, right_full, preferred_element_type=jnp.float32
    ).astype(jnp.bfloat16)
    routed = lax.all_to_all(mixed, "fsdp", split_axis=2, concat_axis=1, tiled=True)
    student = jnp.einsum("nij,jki->njk", routed, left_full, preferred_element_type=jnp.float32)
    inv_root = 1.0 / math.sqrt(group_rows)
    out_grad = (student - target.reshape(student.shape)) * inv_root
    grad_left = jnp.einsum("njk,nij->jki", out_grad, routed.astype(jnp.float32))
    mixed_grad = jnp.einsum("njk,jki->nij", out_grad, left_full.astype(jnp.float32)).astype(
        jnp.bfloat16
    )
    returned = lax.all_to_all(mixed_grad, "fsdp", split_axis=1, concat_axis=2, tiled=True)
    grad_right = jnp.einsum(
        "nik,nij->ikj", returned.astype(jnp.float32), block_input.astype(jnp.float32)
    )
    grad_right, grad_left = (
        lax.psum_scatter(grad_right, "tensor", scatter_dimension=1, tiled=True),
        lax.psum_scatter(grad_left, "tensor", scatter_dimension=1, tiled=True),
    )
    return (grad_right, grad_left)


def layer_kernel(
    n, T, width, cols,
    tok, gw, uw, dw, right, left, gr_out, gl_out,
    wg, wu, wd, pbuf, recv_p, recv_x, hid, t_send, t_recv,
    spread, rload, r_s, rki, lji, rbig, lbig, mix_s, routed, mg_s, mg_r, gr_acc, gr_s, gl_acc, gl_s,
    tok_send, tok_recv, tx_send, tx_recv, tf_send, tf_recv, w_sem, d_sem,
    p_send, p_recv, a_send, a_recv, hx_send, hx_recv, hp_send, hp_recv, r_send, r_recv,
    z_send, z_recv, rf_send, rf_recv, lf_send, lf_recv, mix_send, mix_recv, mg_send, mg_recv,
    gr_send, gr_recv, gl_send, gl_recv,
):
    f32, bf16 = jnp.float32, jnp.bfloat16
    f = lax.axis_index("fsdp")
    z = lax.axis_index("tensor")
    x, c = f // 2, f % 2
    partner = x * 2 + (1 - c)
    across = (1 - x) * 2 + c
    diag = (1 - x) * 2 + (1 - c)
    peers = (across, diag, partner)
    parts, rows, features = spread.shape[0], spread.shape[2], spread.shape[3]
    N = parts * 4 * rows
    G = len(GROUPS)
    ni, nk_local, nj = right.shape
    na = nk_local // T
    nk, nb = left.shape[1] * T, left.shape[2]
    nf = na * ni
    iota = functools.partial(lax.broadcasted_iota, jnp.int32)

    def to(peer):
        return dict(device_id={"fsdp": peer}, device_id_type=MESH)

    def along(peer):
        return dict(device_id={"tensor": peer}, device_id_type=MESH)

    def tile(t):
        return pl.ds(pl.multiple_of(t * width, width), width)

    def token_rows(g):
        return slice(GROUPS[g][0] * 4 * rows, GROUPS[g][1] * 4 * rows)

    def weights(t):
        s = lax.rem(t, DEPTH)
        cc = tile(lax.rem(t, n))
        return (
            pltpu.make_async_copy(gw.at[:, cc], wg.at[s], w_sem.at[0, s]),
            pltpu.make_async_copy(uw.at[:, cc], wu.at[s], w_sem.at[1, s]),
        )

    def feature_columns(peer):
        return pl.ds(pl.multiple_of(peer * features, features), features)

    own = pltpu.make_async_copy(
        tok.at[:, :, feature_columns(f)], spread.at[:, f], tok_send.at[0])
    own.start()
    for t in range(DEPTH - 1):
        for cp in weights(t):
            cp.start()
    load_right = pltpu.make_async_copy(right, rload, rf_send.at[0])
    load_right.start()

    barrier = pltpu.get_barrier_semaphore()
    for peer in peers:
        pl.semaphore_signal(barrier, inc=1, **to(peer))
    for d in range(1, T):
        pl.semaphore_signal(barrier, inc=1, **along(lax.rem(z + d, T)))
    load_right.wait()
    wide_right = rload[...].astype(f32)
    for p in range(T):
        r_s[p] = wide_right[:, p * na:(p + 1) * na].reshape(nf, nj).astype(bf16)

    pl.semaphore_wait(barrier, 3 + T - 1)

    half = lax.rem(z, 2)
    z_mate = z + 1 - 2 * half
    span = parts // 4

    def tok_cross(i, j):
        mm = pl.ds(half * (parts // 2) + j * span, span)
        return pltpu.make_async_remote_copy(
            tok.at[mm, :, feature_columns(peers[i])], spread.at[mm, f],
            tx_send.at[i, j], tx_recv.at[i, j], **to(peers[i]))

    def tok_pass(i, j):
        mm = pl.ds(half * (parts // 2) + j * span, span)
        return pltpu.make_async_remote_copy(
            spread.at[mm, peers[i]], spread.at[mm, peers[i]],
            tf_send.at[i, j], tf_recv.at[i, j], **along(z_mate))

    tok_near = pltpu.make_async_remote_copy(
        tok.at[:, :, feature_columns(partner)], spread.at[:, f],
        tok_send.at[1], tok_recv.at[1], **to(partner))
    tok_near.start()
    pieces = [(i, j) for j in range(2) for i in range(2)]
    for i, j in pieces:
        tok_cross(i, j).start()

    def right_copy(d):
        peer = lax.rem(z + d, T)
        return pltpu.make_async_remote_copy(
            r_s.at[peer], rki.at[z], rf_send.at[d], rf_recv.at[d], **along(peer))

    def left_copy(d):
        peer = lax.rem(z + d, T)
        return pltpu.make_async_remote_copy(
            left.at[pl.ds(peer * na, na)], lji.at[:, z], lf_send.at[d], lf_recv.at[d],
            **along(peer))

    factors = [right_copy(d) for d in range(1, T)] + [left_copy(d) for d in range(1, T)]
    for cp in factors:
        cp.start()
    own_left = pltpu.make_async_copy(left.at[pl.ds(z * na, na)], lji.at[:, z], lf_send.at[0])
    own_left.start()
    rki[z] = r_s[z]

    def pair_copy(p, t):
        cc = tile(t)
        return pltpu.make_async_remote_copy(
            pbuf.at[p, 1 - c, :, :, :, cc], recv_p.at[p, :, :, :, cc],
            p_send.at[p, t], p_recv.at[p, t], **to(partner))

    def pair_sum(p, t):
        pair_copy(p, t).wait_recv()
        cc = tile(t)
        for k in range(2):
            total = pbuf[p, c, :, k, :, cc].astype(f32) + recv_p[p, :, k, :, cc].astype(f32)
            pbuf[p, c, :, k, :, cc] = total.astype(bf16)

    def products(p, t):
        chip = x if p == 0 else 1 - x
        step = p * n + t

        @pl.when(step + DEPTH - 1 < 2 * n)
        def _():
            for cp in weights(step + DEPTH - 1):
                cp.start()

        for cp in weights(step):
            cp.wait()
        s = lax.rem(step, DEPTH)
        toks = spread[:, pl.ds(2 * chip, 2)].reshape(parts * 2 * rows, features)
        cc = tile(t)
        for k, w in ((0, wg), (1, wu)):
            part = jnp.dot(toks, w[s], preferred_element_type=f32).astype(bf16)
            part = part.reshape(parts, 2, rows, width)
            for h in range(2):
                pbuf[p, h, :, k, :, cc] = part[:, h]
        pair_copy(p, t).start()

        @pl.when(t >= 1)
        def _():
            pair_sum(p, t - 1)

    own.wait()
    tok_near.wait_recv()

    def first_half(t, carry):
        products(0, t)
        for q, (i, j) in enumerate(pieces):
            @pl.when(t == 2 * q + 1)
            def _():
                tok_cross(i, j).wait_recv()
                tok_pass(i, j).start()
        return carry

    lax.fori_loop(0, n, first_half, 0)
    pair_sum(0, n - 1)

    def send_a(g):
        mm = slice(*GROUPS[g])
        return pltpu.make_async_remote_copy(
            pbuf.at[0, c, mm], recv_x.at[mm], a_send.at[g], a_recv.at[g], **to(across))

    send_a(0).start()
    send_a(1).start()
    for q, (i, j) in enumerate(pieces):
        if 2 * q + 1 >= n:
            tok_cross(i, j).wait_recv()
            tok_pass(i, j).start()

    own_left.wait()
    for cp in factors:
        cp.wait()
    packed = rki[...].reshape(T * nf, nj)
    lane_block = lax.rem(iota((T * nf, nj), 0), nf) // na
    for i in range(ni):
        rbig[:, i * nj:(i + 1) * nj] = jnp.where(lane_block == i, packed, jnp.zeros_like(packed))
    col = lax.rem(iota((nb, 4 * nf), 1), nf)
    pick = iota((nb, 4 * nf), 0) == (iota((nb, 4 * nf), 1) // nf) * ni + col // na
    wide = jnp.dot(
        lji[...].reshape(na * nk, nb), pick.astype(f32).astype(bf16), preferred_element_type=f32)
    same = iota((na * nk, 4 * nf), 0) // nk == lax.rem(iota((na * nk, 4 * nf), 1), na)
    lbig[...] = jnp.where(same, wide, 0.0).astype(bf16)

    for i, j in pieces:
        tok_pass(i, j).wait_recv()

    def second_half(t, carry):
        products(1, t)
        return carry

    lax.fori_loop(0, n, second_half, 0)
    load_down = pltpu.make_async_copy(dw, wd, d_sem)
    load_down.start()
    pair_sum(1, n - 1)

    mine = pl.ds(pl.multiple_of(f * nf, nf), nf)

    def mix_copy(i):
        return pltpu.make_async_remote_copy(
            mix_s.at[:, pl.ds(pl.multiple_of(peers[i] * nf, nf), nf)],
            routed.at[:, pl.ds(pl.multiple_of(f * nf, nf), nf)],
            mix_send.at[i], mix_recv.at[i], **to(peers[i]))

    def send_hx(g):
        mm = slice(*GROUPS[g])
        return pltpu.make_async_remote_copy(
            hid.at[mm, across], hid.at[mm, across], hx_send.at[g], hx_recv.at[g], **to(across))

    def send_hp(g):
        mm = slice(*GROUPS[g])
        return pltpu.make_async_remote_copy(
            hid.at[mm, across], hid.at[mm, across], hp_send.at[g], hp_recv.at[g], **to(partner))

    def send_r(g):
        mm = slice(*GROUPS[g])
        return pltpu.make_async_remote_copy(
            hid.at[mm, f], hid.at[mm, f], r_send.at[g], r_recv.at[g], **to(partner))

    side = z // 2
    far = 2 * (1 - side)
    inner = (z == 1) | (z == 2)

    def z_near(g, i):
        rr = token_rows(g)
        b = z_mate if i is None else far + i
        k = 0 if i is None else 1 + i
        return pltpu.make_async_remote_copy(
            t_send.at[b, rr], t_recv.at[k, rr], z_send.at[g, k], z_recv.at[g, k],
            **along(z_mate))

    def z_far(g, i):
        rr = token_rows(g)
        return pltpu.make_async_remote_copy(
            t_send.at[far + i, rr], t_recv.at[3, rr], z_send.at[g, 1 + i], z_recv.at[g, 3],
            **along(far + i))

    def mg_copy(g, i):
        rr = token_rows(g)
        return pltpu.make_async_remote_copy(
            mg_s.at[rr, pl.ds(pl.multiple_of(peers[i] * nf, nf), nf)], mg_r.at[f, rr],
            mg_send.at[g, i], mg_recv.at[g, i], **to(peers[i]))

    def make_hidden(g):
        mm = slice(*GROUPS[g])
        send_a(g).wait_recv()

        @pl.loop(0, n)
        def _(t):
            cc = tile(t)
            gate = pbuf[1, c, mm, 0, :, cc].astype(f32) + recv_x[mm, 0, :, cc].astype(f32)
            up = pbuf[1, c, mm, 1, :, cc].astype(f32) + recv_x[mm, 1, :, cc].astype(f32)
            hid[mm, across, :, cc] = (jax.nn.silu(gate) * up).astype(bf16)

        send_hx(g).start()
        send_hp(g).start()

    def make_target(g):
        m0, m1 = GROUPS[g]
        rr = token_rows(g)
        send_hx(g).wait_recv()
        send_r(g).start()
        send_hp(g).wait_recv()
        send_r(g).wait_recv()

        @pl.loop(0, T)
        def _(i):
            b = 2 * lax.rem(side + 1 + i // 2, 2) + lax.rem(i + (i // 2) * (z + 1), 2)
            cc = pl.ds(pl.multiple_of(b * cols, cols), cols)
            h = hid[m0:m1].reshape((m1 - m0) * 4 * rows, n * width)
            t_send[b, rr] = jnp.dot(h, wd[:, cc], preferred_element_type=f32).astype(bf16)

            for k in range(2):
                @pl.when((i == k) & jnp.logical_not(inner))
                def _():
                    z_near(g, k).start()

            @pl.when(i == 2)
            def _():
                z_near(g, None).start()

    def combine(g):
        rr = token_rows(g)

        @pl.when(inner)
        def _():
            for k in range(2):
                z_near(g, k).wait_recv()
                total = t_send[far + k, rr].astype(f32) + t_recv[1 + k, rr].astype(f32)
                t_send[far + k, rr] = total.astype(bf16)
                z_far(g, k).start()

    def make_grads(g, first):
        rr = token_rows(g)
        student = lax.dot_general(
            routed[rr], lbig[...], (((1,), (1,)), ((), ())), preferred_element_type=f32)
        z_near(g, None).wait_recv()
        z_far(g, 0).wait_recv()
        tgt = t_send[z, rr].astype(f32) + t_recv[0, rr].astype(f32) + t_recv[3, rr].astype(f32)
        out_grad = (student - tgt) * (1.0 / math.sqrt(N))
        mg_s[rr] = jnp.dot(
            out_grad.astype(bf16), lbig[...], preferred_element_type=f32).astype(bf16)
        for i in range(3):
            mg_copy(g, i).start()
        mg_r[f, rr] = mg_s[rr, mine]
        part = jnp.dot(out_grad.T.astype(bf16), routed[rr], preferred_element_type=f32)
        if first:
            gl_acc[...] = part
        else:
            gl_acc[...] += part

    row_block = iota((nf, nj), 0) // na

    def right_terms(b, m0, m1):
        rr = slice(m0 * 4 * rows, m1 * 4 * rows)
        flipped = mg_r[b, rr].astype(f32).T.astype(bf16)
        total = jnp.zeros((nf, nj), f32)
        for i in range(0, ni, 2):
            rhs = spread[m0:m1, :, :, i * nj:(i + 2) * nj].reshape((m1 - m0) * 4 * rows, 2 * nj)
            part = jnp.dot(flipped, rhs, preferred_element_type=f32)
            for k in range(2):
                total += jnp.where(row_block == i + k, part[:, k * nj:(k + 1) * nj], 0.0)
        return total

    def make_mixed():
        mix_s[...] = lax.dot_general(
            spread[...].reshape(N, features), rbig[...], (((1,), (1,)), ((), ())),
            preferred_element_type=f32).astype(bf16)
        for i in range(3):
            mix_copy(i).start()
        routed[:, mine] = mix_s[:, mine]

    def wait_mixed():
        for i in range(3):
            mix_copy(i).wait_recv()

    early = GROUPS[LATE][0]

    def early_right():
        for g in range(LATE):
            for i in range(3):
                mg_copy(g, i).wait_recv()

        @pl.loop(0, 4)
        def _(b):
            gr_acc[b] = right_terms(b, 0, early)

    stages = {
        "a": lambda g: send_a(g).start(),
        "h": make_hidden,
        "m": lambda g: make_mixed(),
        "w": lambda g: wait_mixed(),
        "d": lambda g: load_down.wait(),
        "t": make_target,
        "c": combine,
        "g": lambda g: make_grads(g, g == 0),
        "r": lambda g: early_right(),
    }
    for step in PLAN.split():
        stages[step[0]](int(step[1:] or 0))

    def gl_copy(d):
        peer = lax.rem(z + d, T)
        return pltpu.make_async_remote_copy(
            gl_s.at[:, peer], gl_out.at[pl.ds(z * na, na)], gl_send.at[d], gl_recv.at[d],
            **along(peer))

    def gr_copy(b):
        return pltpu.make_async_remote_copy(
            gr_s.at[b], gr_out.at[z], gr_send.at[b], gr_recv.at[z], **along(b))

    shape = (na * nk, 4 * nf)
    keep = iota(shape, 0) // nk == lax.rem(iota(shape, 1), na)
    fold = iota((4 * nf, nb), 1) == (iota((4 * nf, nb), 0) // nf) * ni + lax.rem(
        iota((4 * nf, nb), 0), nf) // na
    total = jnp.dot(
        jnp.where(keep, gl_acc[...], 0.0).astype(bf16), fold.astype(f32).astype(bf16),
        preferred_element_type=f32)
    gl_s[...] = total.astype(bf16).reshape(na, T, nk // T, nb)
    for d in range(1, T):
        gl_copy(d).start()
    gl_out[pl.ds(z * na, na)] = gl_s[:, z]

    def finish_right(b):
        gr_s[b] = (gr_acc[b] + right_terms(b, early, parts)).astype(bf16)

        @pl.when(b != z)
        def _():
            gr_copy(b).start()

        @pl.when(b == z)
        def _():
            gr_out[z] = gr_s[b]

    finish_right(f)
    for i in (2, 0, 1):
        for g in range(LATE, G):
            mg_copy(g, i).wait_recv()
        finish_right(peers[i])

    for d in range(1, T):
        gl_copy(d).wait()
    for b in range(T):
        @pl.when(z != b)
        def _():
            gr_copy(b).wait_send()
            pltpu.make_async_remote_copy(
                gr_s.at[b], gr_out.at[b], gr_send.at[b], gr_recv.at[b], **along(b)).wait_recv()

    tok_near.wait_send()
    for i, j in pieces:
        tok_cross(i, j).wait_send()
        tok_pass(i, j).wait_send()
    for i in range(3):
        mix_copy(i).wait_send()
    for g in range(G):
        for cp in (send_a(g), send_hx(g), send_hp(g), send_r(g)):
            cp.wait_send()
        z_near(g, None).wait_send()
        for k in range(2):
            @pl.when(inner)
            def _():
                z_far(g, k).wait_send()

            @pl.when(jnp.logical_not(inner))
            def _():
                z_near(g, k).wait_send()

        for i in range(3):
            mg_copy(g, i).wait_send()

    def drain(t, carry):
        for p in range(2):
            pair_copy(p, t).wait_send()
        return carry

    lax.fori_loop(0, n, drain, 0)


def fused_body(tokens, gate_weight, up_weight, down_weight, right_factor, left_factor):
    T = lax.axis_size("tensor")
    rows = SUB
    parts = tokens.shape[0] // rows
    tok = tokens.reshape(parts, rows, tokens.shape[1])
    features, hidden = gate_weight.shape
    width = CHUNK
    n = hidden // width
    G = len(GROUPS)
    cols = down_weight.shape[1] // T
    bf16, f32 = jnp.bfloat16, jnp.float32
    dma = pltpu.SemaphoreType.DMA
    anyspace = pl.BlockSpec(memory_space=pl.ANY)
    vmem = pl.BlockSpec(memory_space=pltpu.VMEM)
    ni, nkr, nj = right_factor.shape
    na, nkl, nb = left_factor.shape[0] // T, left_factor.shape[1], left_factor.shape[2]
    nf, nk = na * ni, nkl * T
    N = 4 * parts * rows
    right_parts, left_parts = pl.pallas_call(
        functools.partial(layer_kernel, n, T, width, cols),
        out_shape=(
            jax.ShapeDtypeStruct((T, nf, nj), bf16),
            jax.ShapeDtypeStruct((T * na, nkl, nb), bf16),
        ),
        in_specs=[anyspace] * 6,
        out_specs=(vmem, vmem),
        scratch_shapes=[
            pltpu.VMEM((DEPTH, features, width), bf16),
            pltpu.VMEM((DEPTH, features, width), bf16),
            pltpu.VMEM((hidden, T * cols), bf16),
            pltpu.VMEM((2, 2, parts, 2, rows, hidden), bf16),
            pltpu.VMEM((2, parts, 2, rows, hidden), bf16),
            pltpu.VMEM((parts, 2, rows, hidden), bf16),
            pltpu.VMEM((parts, 4, rows, hidden), bf16),
            pltpu.VMEM((T, N, cols), bf16),
            pltpu.VMEM((4, N, cols), bf16),
            pltpu.VMEM((parts, 4, rows, features), bf16),
            pltpu.VMEM((ni, nkr, nj), bf16),
            pltpu.VMEM((T, nf, nj), bf16),
            pltpu.VMEM((T, nf, nj), bf16),
            pltpu.VMEM((na, T, nkl, nb), bf16),
            pltpu.VMEM((4 * nf, features), bf16),
            pltpu.VMEM((na * nk, 4 * nf), bf16),
            pltpu.VMEM((N, 4 * nf), bf16),
            pltpu.VMEM((N, 4 * nf), bf16),
            pltpu.VMEM((N, 4 * nf), bf16),
            pltpu.VMEM((4, N, nf), bf16),
            pltpu.VMEM((4, nf, nj), f32),
            pltpu.VMEM((4, nf, nj), bf16),
            pltpu.VMEM((na * nk, 4 * nf), f32),
            pltpu.VMEM((na, T, nkl, nb), bf16),
            dma((2,)), dma((2,)), dma((2, 2)), dma((2, 2)), dma((2, 2)), dma((2, 2)),
            dma((2, DEPTH)), dma,
            dma((2, n)), dma((2, n)), dma((G,)), dma((G,)),
            dma((G,)), dma((G,)), dma((G,)), dma((G,)), dma((G,)), dma((G,)),
            dma((G, 3)), dma((G, 4)),
            dma((T,)), dma((T,)), dma((T,)), dma((T,)),
            dma((3,)), dma((3,)), dma((G, 3)), dma((G, 3)),
            dma((T,)), dma((T,)), dma((T,)), dma((T,)),
        ],
        compiler_params=pltpu.CompilerParams(
            collective_id=0, has_side_effects=True, vmem_limit_bytes=62 * 1024 * 1024
        ),
        name="layer",
    )(tok, gate_weight, up_weight, down_weight, right_factor, left_factor)

    def widen(right_ref, left_ref, right_out, left_out):
        for t in range(T):
            right_out[:, t * na:(t + 1) * na] = right_ref[t].astype(f32).reshape(ni, na, nj)
        left_out[...] = left_ref[...].astype(f32)

    return pl.pallas_call(
        widen,
        out_shape=(
            jax.ShapeDtypeStruct((ni, nkr, nj), f32),
            jax.ShapeDtypeStruct((T * na, nkl, nb), f32),
        ),
        in_specs=[vmem] * 2,
        out_specs=(vmem, vmem),
        name="widen",
    )(right_parts, left_parts)


def body(tokens, gate_weight, up_weight, down_weight, right_factor, left_factor):
    F, T = lax.axis_size("fsdp"), lax.axis_size("tensor")
    fits = (
        F == 4
        and T == 4
        and gate_weight.shape[1] % CHUNK == 0
        and left_factor.shape[0] % T == 0
        and right_factor.shape[1] % T == 0
        and gate_weight.shape[0] <= 2048
        and tokens.shape[0] == 128
    )
    run = fused_body if fits else plain_body
    return run(tokens, gate_weight, up_weight, down_weight, right_factor, left_factor)


def solution(mesh):
    return jax.shard_map(
        body,
        mesh=mesh,
        in_specs=(
            P(("groups", "fsdp"), None),
            P("fsdp", "tensor"),
            P("fsdp", "tensor"),
            P("tensor", "fsdp"),
            P("fsdp", "tensor", None),
            P("fsdp", "tensor", None),
        ),
        out_specs=(P(("groups", "fsdp"), "tensor", None), P(("groups", "fsdp"), "tensor", None)),
        check_vma=False,
    )
```

```python
import functools
import math

import jax
import jax.numpy as jnp
from jax import lax
from jax.experimental import pallas as pl
from jax.experimental.pallas import tpu as pltpu
from jax.sharding import PartitionSpec as P

MESH = pl.DeviceIdType.MESH
CHUNK = 512
SUB = 16
GROUPS = ((0, 2), (2, 4), (4, 6), (6, 7), (7, 8))
DEPTH = 3
LATE = 3
PLAN = (
    "h0", "h1", "a2", "m", "d", "t0", "t1", "c0", "c1", "h2",
    "a3", "a4", "w", "g0", "g1", "t2", "h3", "c2", "h4", "g2",
    "t3", "t4", "c3", "c4", "r", "g3", "g4",
)


def plain_body(tokens, gate_weight, up_weight, down_weight, right_factor, left_factor):
    fsdp_count = lax.axis_size("fsdp")
    tensor_count = lax.axis_size("tensor")
    tok_local = tokens.shape[0]
    group_rows = tok_local * fsdp_count
    share_rows = group_rows // tensor_count
    hid_local = gate_weight.shape[1]
    spread = lax.all_to_all(tokens, "fsdp", split_axis=1, concat_axis=0, tiled=True)
    student_in = lax.dynamic_slice_in_dim(
        spread, lax.axis_index("tensor") * share_rows, share_rows, 0
    )
    gate_part = jnp.dot(spread, gate_weight, preferred_element_type=jnp.float32)
    up_part = jnp.dot(spread, up_weight, preferred_element_type=jnp.float32)
    partial_value = jnp.concatenate([gate_part, up_part], axis=1)
    summed = lax.psum(partial_value.astype(jnp.bfloat16), "fsdp").astype(jnp.float32)
    hidden = (jax.nn.silu(summed[:, :hid_local]) * summed[:, hid_local:]).astype(jnp.bfloat16)
    target = lax.psum_scatter(
        jnp.dot(hidden, down_weight, preferred_element_type=jnp.float32).astype(jnp.bfloat16),
        "tensor",
        scatter_dimension=0,
        tiled=True,
    ).astype(jnp.float32)
    right_full, left_full = (
        lax.all_gather(right_factor, "tensor", axis=1, tiled=True),
        lax.all_gather(left_factor, "tensor", axis=1, tiled=True),
    )
    blocks_local = right_full.shape[0]
    block_size = right_full.shape[2]
    block_input = student_in.reshape(share_rows, blocks_local, block_size)
    mixed = jnp.einsum(
        "nij,ikj->nik", block_input, right_full, preferred_element_type=jnp.float32
    ).astype(jnp.bfloat16)
    routed = lax.all_to_all(mixed, "fsdp", split_axis=2, concat_axis=1, tiled=True)
    student = jnp.einsum("nij,jki->njk", routed, left_full, preferred_element_type=jnp.float32)
    inv_root = 1.0 / math.sqrt(group_rows)
    out_grad = (student - target.reshape(student.shape)) * inv_root
    grad_left = jnp.einsum("njk,nij->jki", out_grad, routed.astype(jnp.float32))
    mixed_grad = jnp.einsum("njk,jki->nij", out_grad, left_full.astype(jnp.float32)).astype(
        jnp.bfloat16
    )
    returned = lax.all_to_all(mixed_grad, "fsdp", split_axis=1, concat_axis=2, tiled=True)
    grad_right = jnp.einsum(
        "nik,nij->ikj", returned.astype(jnp.float32), block_input.astype(jnp.float32)
    )
    grad_right, grad_left = (
        lax.psum_scatter(grad_right, "tensor", scatter_dimension=1, tiled=True),
        lax.psum_scatter(grad_left, "tensor", scatter_dimension=1, tiled=True),
    )
    return (grad_right, grad_left)


def layer_kernel(
    n, T, width, cols,
    tok, gw, uw, dw, right, left, gr_out, gl_out,
    wg, wu, wd, pbuf, recv_p, recv_x, hid, t_send, t_recv,
    spread, rload, r_s, rki, lji, rbig, lbig, mix_s, routed, mg_s, mg_r, gr_acc, gr_s, gl_acc, gl_s,
    tok_send, tok_recv, tx_send, tx_recv, tf_send, tf_recv, w_sem, d_sem,
    p_send, p_recv, a_send, a_recv, hx_send, hx_recv, hp_send, hp_recv, r_send, r_recv,
    z_send, z_recv, rf_send, rf_recv, lf_send, lf_recv, mix_send, mix_recv, mg_send, mg_recv,
    gr_send, gr_recv, gl_send, gl_recv,
):
    f32, bf16 = jnp.float32, jnp.bfloat16
    f = lax.axis_index("fsdp")
    z = lax.axis_index("tensor")
    x, c = f // 2, f % 2
    partner = x * 2 + (1 - c)
    across = (1 - x) * 2 + c
    diag = (1 - x) * 2 + (1 - c)
    peers = (across, diag, partner)
    parts, rows, features = spread.shape[0], spread.shape[2], spread.shape[3]
    N = parts * 4 * rows
    G = len(GROUPS)
    ni, nk_local, nj = right.shape
    na = nk_local // T
    nk, nb = left.shape[1] * T, left.shape[2]
    nf = na * ni
    iota = functools.partial(lax.broadcasted_iota, jnp.int32)

    def to(peer):
        return dict(device_id={"fsdp": peer}, device_id_type=MESH)

    def along(peer):
        return dict(device_id={"tensor": peer}, device_id_type=MESH)

    def tile(t):
        return pl.ds(pl.multiple_of(t * width, width), width)

    def token_rows(g):
        return slice(GROUPS[g][0] * 4 * rows, GROUPS[g][1] * 4 * rows)

    def weights(t):
        s = lax.rem(t, DEPTH)
        cc = tile(lax.rem(t, n))
        return (
            pltpu.make_async_copy(gw.at[:, cc], wg.at[s], w_sem.at[0, s]),
            pltpu.make_async_copy(uw.at[:, cc], wu.at[s], w_sem.at[1, s]),
        )

    def feature_columns(peer):
        return pl.ds(pl.multiple_of(peer * features, features), features)

    own = pltpu.make_async_copy(
        tok.at[:, :, feature_columns(f)], spread.at[:, f], tok_send.at[0])
    own.start()
    for t in range(DEPTH - 1):
        for cp in weights(t):
            cp.start()
    load_right = pltpu.make_async_copy(right, rload, rf_send.at[0])
    load_right.start()

    barrier = pltpu.get_barrier_semaphore()
    for peer in peers:
        pl.semaphore_signal(barrier, inc=1, **to(peer))
    for d in range(1, T):
        pl.semaphore_signal(barrier, inc=1, **along(lax.rem(z + d, T)))
    load_right.wait()
    wide_right = rload[...].astype(f32)
    for p in range(T):
        r_s[p] = wide_right[:, p * na:(p + 1) * na].reshape(nf, nj).astype(bf16)

    pl.semaphore_wait(barrier, 3 + T - 1)

    half = lax.rem(z, 2)
    z_mate = z + 1 - 2 * half
    span = parts // 4

    def tok_cross(i, j):
        mm = pl.ds(half * (parts // 2) + j * span, span)
        return pltpu.make_async_remote_copy(
            tok.at[mm, :, feature_columns(peers[i])], spread.at[mm, f],
            tx_send.at[i, j], tx_recv.at[i, j], **to(peers[i]))

    def tok_pass(i, j):
        mm = pl.ds(half * (parts // 2) + j * span, span)
        return pltpu.make_async_remote_copy(
            spread.at[mm, peers[i]], spread.at[mm, peers[i]],
            tf_send.at[i, j], tf_recv.at[i, j], **along(z_mate))

    tok_near = pltpu.make_async_remote_copy(
        tok.at[:, :, feature_columns(partner)], spread.at[:, f],
        tok_send.at[1], tok_recv.at[1], **to(partner))
    tok_near.start()
    pieces = [(i, j) for j in range(2) for i in range(2)]
    for i, j in pieces:
        tok_cross(i, j).start()

    def right_copy(d):
        peer = lax.rem(z + d, T)
        return pltpu.make_async_remote_copy(
            r_s.at[peer], rki.at[z], rf_send.at[d], rf_recv.at[d], **along(peer))

    def left_copy(d):
        peer = lax.rem(z + d, T)
        return pltpu.make_async_remote_copy(
            left.at[pl.ds(peer * na, na)], lji.at[:, z], lf_send.at[d], lf_recv.at[d],
            **along(peer))

    factors = [right_copy(d) for d in range(1, T)] + [left_copy(d) for d in range(1, T)]
    for cp in factors:
        cp.start()
    own_left = pltpu.make_async_copy(left.at[pl.ds(z * na, na)], lji.at[:, z], lf_send.at[0])
    own_left.start()
    rki[z] = r_s[z]

    def pair_copy(p, t):
        cc = tile(t)
        return pltpu.make_async_remote_copy(
            pbuf.at[p, 1 - c, :, :, :, cc], recv_p.at[p, :, :, :, cc],
            p_send.at[p, t], p_recv.at[p, t], **to(partner))

    def pair_sum(p, t):
        pair_copy(p, t).wait_recv()
        cc = tile(t)
        for k in range(2):
            total = pbuf[p, c, :, k, :, cc].astype(f32) + recv_p[p, :, k, :, cc].astype(f32)
            pbuf[p, c, :, k, :, cc] = total.astype(bf16)

    def products(p, t):
        chip = x if p == 0 else 1 - x
        step = p * n + t

        @pl.when(step + DEPTH - 1 < 2 * n)
        def _():
            for cp in weights(step + DEPTH - 1):
                cp.start()

        for cp in weights(step):
            cp.wait()
        s = lax.rem(step, DEPTH)
        toks = spread[:, pl.ds(2 * chip, 2)].reshape(parts * 2 * rows, features)
        cc = tile(t)
        for k, w in ((0, wg), (1, wu)):
            part = jnp.dot(toks, w[s], preferred_element_type=f32).astype(bf16)
            part = part.reshape(parts, 2, rows, width)
            for h in range(2):
                pbuf[p, h, :, k, :, cc] = part[:, h]
        pair_copy(p, t).start()

        @pl.when(t >= 1)
        def _():
            pair_sum(p, t - 1)

    own.wait()
    tok_near.wait_recv()

    def first_half(t, carry):
        products(0, t)
        for q, (i, j) in enumerate(pieces):
            @pl.when(t == 2 * q + 1)
            def _():
                tok_cross(i, j).wait_recv()
                tok_pass(i, j).start()
        return carry

    lax.fori_loop(0, n, first_half, 0)
    pair_sum(0, n - 1)

    def send_a(g):
        mm = slice(*GROUPS[g])
        return pltpu.make_async_remote_copy(
            pbuf.at[0, c, mm], recv_x.at[mm], a_send.at[g], a_recv.at[g], **to(across))

    send_a(0).start()
    send_a(1).start()
    for q, (i, j) in enumerate(pieces):
        if 2 * q + 1 >= n:
            tok_cross(i, j).wait_recv()
            tok_pass(i, j).start()

    own_left.wait()
    for cp in factors:
        cp.wait()
    packed = rki[...].reshape(T * nf, nj)
    lane_block = lax.rem(iota((T * nf, nj), 0), nf) // na
    for i in range(ni):
        rbig[:, i * nj:(i + 1) * nj] = jnp.where(lane_block == i, packed, jnp.zeros_like(packed))
    col = lax.rem(iota((nb, 4 * nf), 1), nf)
    pick = iota((nb, 4 * nf), 0) == (iota((nb, 4 * nf), 1) // nf) * ni + col // na
    wide = jnp.dot(
        lji[...].reshape(na * nk, nb), pick.astype(f32).astype(bf16), preferred_element_type=f32)
    same = iota((na * nk, 4 * nf), 0) // nk == lax.rem(iota((na * nk, 4 * nf), 1), na)
    lbig[...] = jnp.where(same, wide, 0.0).astype(bf16)

    for i, j in pieces:
        tok_pass(i, j).wait_recv()

    def second_half(t, carry):
        products(1, t)
        return carry

    lax.fori_loop(0, n, second_half, 0)
    load_down = pltpu.make_async_copy(dw, wd, d_sem)
    load_down.start()
    pair_sum(1, n - 1)

    mine = pl.ds(pl.multiple_of(f * nf, nf), nf)

    def mix_copy(i):
        return pltpu.make_async_remote_copy(
            mix_s.at[:, pl.ds(pl.multiple_of(peers[i] * nf, nf), nf)],
            routed.at[:, pl.ds(pl.multiple_of(f * nf, nf), nf)],
            mix_send.at[i], mix_recv.at[i], **to(peers[i]))

    def send_hx(g):
        mm = slice(*GROUPS[g])
        return pltpu.make_async_remote_copy(
            hid.at[mm, across], hid.at[mm, across], hx_send.at[g], hx_recv.at[g], **to(across))

    def send_hp(g):
        mm = slice(*GROUPS[g])
        return pltpu.make_async_remote_copy(
            hid.at[mm, across], hid.at[mm, across], hp_send.at[g], hp_recv.at[g], **to(partner))

    def send_r(g):
        mm = slice(*GROUPS[g])
        return pltpu.make_async_remote_copy(
            hid.at[mm, f], hid.at[mm, f], r_send.at[g], r_recv.at[g], **to(partner))

    side = z // 2
    far = 2 * (1 - side)
    inner = (z == 1) | (z == 2)

    def z_near(g, i):
        rr = token_rows(g)
        b = z_mate if i is None else far + i
        k = 0 if i is None else 1 + i
        return pltpu.make_async_remote_copy(
            t_send.at[b, rr], t_recv.at[k, rr], z_send.at[g, k], z_recv.at[g, k],
            **along(z_mate))

    def z_far(g, i):
        rr = token_rows(g)
        return pltpu.make_async_remote_copy(
            t_send.at[far + i, rr], t_recv.at[3, rr], z_send.at[g, 1 + i], z_recv.at[g, 3],
            **along(far + i))

    def mg_copy(g, i):
        rr = token_rows(g)
        return pltpu.make_async_remote_copy(
            mg_s.at[rr, pl.ds(pl.multiple_of(peers[i] * nf, nf), nf)], mg_r.at[f, rr],
            mg_send.at[g, i], mg_recv.at[g, i], **to(peers[i]))

    def make_hidden(g):
        mm = slice(*GROUPS[g])
        send_a(g).wait_recv()

        @pl.loop(0, n)
        def _(t):
            cc = tile(t)
            gate = pbuf[1, c, mm, 0, :, cc].astype(f32) + recv_x[mm, 0, :, cc].astype(f32)
            up = pbuf[1, c, mm, 1, :, cc].astype(f32) + recv_x[mm, 1, :, cc].astype(f32)
            hid[mm, across, :, cc] = (jax.nn.silu(gate) * up).astype(bf16)

        send_hx(g).start()
        send_hp(g).start()

    def make_target(g):
        m0, m1 = GROUPS[g]
        rr = token_rows(g)
        send_hx(g).wait_recv()
        send_r(g).start()
        send_hp(g).wait_recv()
        send_r(g).wait_recv()

        @pl.loop(0, T)
        def _(i):
            b = 2 * lax.rem(side + 1 + i // 2, 2) + lax.rem(i + (i // 2) * (z + 1), 2)
            cc = pl.ds(pl.multiple_of(b * cols, cols), cols)
            h = hid[m0:m1].reshape((m1 - m0) * 4 * rows, n * width)
            t_send[b, rr] = jnp.dot(h, wd[:, cc], preferred_element_type=f32).astype(bf16)

            for k in range(2):
                @pl.when((i == k) & jnp.logical_not(inner))
                def _():
                    z_near(g, k).start()

            @pl.when(i == 2)
            def _():
                z_near(g, None).start()

    def combine(g):
        rr = token_rows(g)

        @pl.when(inner)
        def _():
            for k in range(2):
                z_near(g, k).wait_recv()
                total = t_send[far + k, rr].astype(f32) + t_recv[1 + k, rr].astype(f32)
                t_send[far + k, rr] = total.astype(bf16)
                z_far(g, k).start()

    def make_grads(g, first):
        rr = token_rows(g)
        student = lax.dot_general(
            routed[rr], lbig[...], (((1,), (1,)), ((), ())), preferred_element_type=f32)
        z_near(g, None).wait_recv()
        z_far(g, 0).wait_recv()
        tgt = t_send[z, rr].astype(f32) + t_recv[0, rr].astype(f32) + t_recv[3, rr].astype(f32)
        out_grad = (student - tgt) * (1.0 / math.sqrt(N))
        mg_s[rr] = jnp.dot(
            out_grad.astype(bf16), lbig[...], preferred_element_type=f32).astype(bf16)
        for i in range(3):
            mg_copy(g, i).start()
        mg_r[f, rr] = mg_s[rr, mine]
        part = jnp.dot(out_grad.T.astype(bf16), routed[rr], preferred_element_type=f32)
        if first:
            gl_acc[...] = part
        else:
            gl_acc[...] += part

    row_block = iota((nf, nj), 0) // na

    def right_terms(b, m0, m1):
        rr = slice(m0 * 4 * rows, m1 * 4 * rows)
        flipped = mg_r[b, rr].astype(f32).T.astype(bf16)
        total = jnp.zeros((nf, nj), f32)
        for i in range(0, ni, 2):
            rhs = spread[m0:m1, :, :, i * nj:(i + 2) * nj].reshape((m1 - m0) * 4 * rows, 2 * nj)
            part = jnp.dot(flipped, rhs, preferred_element_type=f32)
            for k in range(2):
                total += jnp.where(row_block == i + k, part[:, k * nj:(k + 1) * nj], 0.0)
        return total

    def make_mixed():
        mix_s[...] = lax.dot_general(
            spread[...].reshape(N, features), rbig[...], (((1,), (1,)), ((), ())),
            preferred_element_type=f32).astype(bf16)
        for i in range(3):
            mix_copy(i).start()
        routed[:, mine] = mix_s[:, mine]

    def wait_mixed():
        for i in range(3):
            mix_copy(i).wait_recv()

    early = GROUPS[LATE][0]

    def early_right():
        for g in range(LATE):
            for i in range(3):
                mg_copy(g, i).wait_recv()

        @pl.loop(0, 4)
        def _(b):
            gr_acc[b] = right_terms(b, 0, early)

    stages = {
        "a": lambda g: send_a(g).start(),
        "h": make_hidden,
        "m": lambda g: make_mixed(),
        "w": lambda g: wait_mixed(),
        "d": lambda g: load_down.wait(),
        "t": make_target,
        "c": combine,
        "g": lambda g: make_grads(g, g == 0),
        "r": lambda g: early_right(),
    }
    for step in PLAN:
        stages[step[0]](int(step[1:] or 0))

    def gl_copy(d):
        peer = lax.rem(z + d, T)
        return pltpu.make_async_remote_copy(
            gl_s.at[:, peer], gl_out.at[pl.ds(z * na, na)], gl_send.at[d], gl_recv.at[d],
            **along(peer))

    def gr_copy(b):
        return pltpu.make_async_remote_copy(
            gr_s.at[b], gr_out.at[z], gr_send.at[b], gr_recv.at[z], **along(b))

    shape = (na * nk, 4 * nf)
    keep = iota(shape, 0) // nk == lax.rem(iota(shape, 1), na)
    fold = iota((4 * nf, nb), 1) == (iota((4 * nf, nb), 0) // nf) * ni + lax.rem(
        iota((4 * nf, nb), 0), nf) // na
    total = jnp.dot(
        jnp.where(keep, gl_acc[...], 0.0).astype(bf16), fold.astype(f32).astype(bf16),
        preferred_element_type=f32)
    gl_s[...] = total.astype(bf16).reshape(na, T, nk // T, nb)
    for d in range(1, T):
        gl_copy(d).start()
    gl_out[pl.ds(z * na, na)] = gl_s[:, z]

    def finish_right(b):
        gr_s[b] = (gr_acc[b] + right_terms(b, early, parts)).astype(bf16)

        @pl.when(b != z)
        def _():
            gr_copy(b).start()

        @pl.when(b == z)
        def _():
            gr_out[z] = gr_s[b]

    finish_right(f)
    for i in (2, 0, 1):
        for g in range(LATE, G):
            mg_copy(g, i).wait_recv()
        finish_right(peers[i])

    for d in range(1, T):
        gl_copy(d).wait()
    for b in range(T):
        @pl.when(z != b)
        def _():
            gr_copy(b).wait_send()
            pltpu.make_async_remote_copy(
                gr_s.at[b], gr_out.at[b], gr_send.at[b], gr_recv.at[b], **along(b)).wait_recv()

    tok_near.wait_send()
    for i, j in pieces:
        tok_cross(i, j).wait_send()
        tok_pass(i, j).wait_send()
    for i in range(3):
        mix_copy(i).wait_send()
    for g in range(G):
        for cp in (send_a(g), send_hx(g), send_hp(g), send_r(g)):
            cp.wait_send()
        z_near(g, None).wait_send()
        for k in range(2):
            @pl.when(inner)
            def _():
                z_far(g, k).wait_send()

            @pl.when(jnp.logical_not(inner))
            def _():
                z_near(g, k).wait_send()

        for i in range(3):
            mg_copy(g, i).wait_send()

    def drain(t, carry):
        for p in range(2):
            pair_copy(p, t).wait_send()
        return carry

    lax.fori_loop(0, n, drain, 0)


def fused_body(tokens, gate_weight, up_weight, down_weight, right_factor, left_factor):
    T = lax.axis_size("tensor")
    rows = SUB
    parts = tokens.shape[0] // rows
    tok = tokens.reshape(parts, rows, tokens.shape[1])
    features, hidden = gate_weight.shape
    width = CHUNK
    n = hidden // width
    G = len(GROUPS)
    cols = down_weight.shape[1] // T
    bf16, f32 = jnp.bfloat16, jnp.float32
    dma = pltpu.SemaphoreType.DMA
    anyspace = pl.BlockSpec(memory_space=pl.ANY)
    vmem = pl.BlockSpec(memory_space=pltpu.VMEM)
    ni, nkr, nj = right_factor.shape
    na, nkl, nb = left_factor.shape[0] // T, left_factor.shape[1], left_factor.shape[2]
    nf, nk = na * ni, nkl * T
    N = 4 * parts * rows
    right_parts, left_parts = pl.pallas_call(
        functools.partial(layer_kernel, n, T, width, cols),
        out_shape=(
            jax.ShapeDtypeStruct((T, nf, nj), bf16),
            jax.ShapeDtypeStruct((T * na, nkl, nb), bf16),
        ),
        in_specs=[anyspace] * 6,
        out_specs=(vmem, vmem),
        scratch_shapes=[
            pltpu.VMEM((DEPTH, features, width), bf16),
            pltpu.VMEM((DEPTH, features, width), bf16),
            pltpu.VMEM((hidden, T * cols), bf16),
            pltpu.VMEM((2, 2, parts, 2, rows, hidden), bf16),
            pltpu.VMEM((2, parts, 2, rows, hidden), bf16),
            pltpu.VMEM((parts, 2, rows, hidden), bf16),
            pltpu.VMEM((parts, 4, rows, hidden), bf16),
            pltpu.VMEM((T, N, cols), bf16),
            pltpu.VMEM((4, N, cols), bf16),
            pltpu.VMEM((parts, 4, rows, features), bf16),
            pltpu.VMEM((ni, nkr, nj), bf16),
            pltpu.VMEM((T, nf, nj), bf16),
            pltpu.VMEM((T, nf, nj), bf16),
            pltpu.VMEM((na, T, nkl, nb), bf16),
            pltpu.VMEM((4 * nf, features), bf16),
            pltpu.VMEM((na * nk, 4 * nf), bf16),
            pltpu.VMEM((N, 4 * nf), bf16),
            pltpu.VMEM((N, 4 * nf), bf16),
            pltpu.VMEM((N, 4 * nf), bf16),
            pltpu.VMEM((4, N, nf), bf16),
            pltpu.VMEM((4, nf, nj), f32),
            pltpu.VMEM((4, nf, nj), bf16),
            pltpu.VMEM((na * nk, 4 * nf), f32),
            pltpu.VMEM((na, T, nkl, nb), bf16),
            dma((2,)), dma((2,)), dma((2, 2)), dma((2, 2)), dma((2, 2)), dma((2, 2)),
            dma((2, DEPTH)), dma,
            dma((2, n)), dma((2, n)), dma((G,)), dma((G,)),
            dma((G,)), dma((G,)), dma((G,)), dma((G,)), dma((G,)), dma((G,)),
            dma((G, 3)), dma((G, 4)),
            dma((T,)), dma((T,)), dma((T,)), dma((T,)),
            dma((3,)), dma((3,)), dma((G, 3)), dma((G, 3)),
            dma((T,)), dma((T,)), dma((T,)), dma((T,)),
        ],
        compiler_params=pltpu.CompilerParams(
            collective_id=0, has_side_effects=True, vmem_limit_bytes=62 * 1024 * 1024
        ),
        name="layer",
    )(tok, gate_weight, up_weight, down_weight, right_factor, left_factor)

    def widen(right_ref, left_ref, right_out, left_out):
        for t in range(T):
            right_out[:, t * na:(t + 1) * na] = right_ref[t].astype(f32).reshape(ni, na, nj)
        left_out[...] = left_ref[...].astype(f32)

    return pl.pallas_call(
        widen,
        out_shape=(
            jax.ShapeDtypeStruct((ni, nkr, nj), f32),
            jax.ShapeDtypeStruct((T * na, nkl, nb), f32),
        ),
        in_specs=[vmem] * 2,
        out_specs=(vmem, vmem),
        name="widen",
    )(right_parts, left_parts)


def body(tokens, gate_weight, up_weight, down_weight, right_factor, left_factor):
    F, T = lax.axis_size("fsdp"), lax.axis_size("tensor")
    fits = (
        F == 4
        and T == 4
        and gate_weight.shape[1] % CHUNK == 0
        and left_factor.shape[0] % T == 0
        and right_factor.shape[1] % T == 0
        and gate_weight.shape[0] <= 2048
        and tokens.shape[0] == 128
    )
    run = fused_body if fits else plain_body
    return run(tokens, gate_weight, up_weight, down_weight, right_factor, left_factor)


def solution(mesh):
    return jax.shard_map(
        body,
        mesh=mesh,
        in_specs=(
            P(("groups", "fsdp"), None),
            P("fsdp", "tensor"),
            P("fsdp", "tensor"),
            P("tensor", "fsdp"),
            P("fsdp", "tensor", None),
            P("fsdp", "tensor", None),
        ),
        out_specs=(P(("groups", "fsdp"), "tensor", None), P(("groups", "fsdp"), "tensor", None)),
        check_vma=False,
    )
```

```python
import functools
import math

import jax
import jax.numpy as jnp
from jax import lax
from jax.experimental import pallas as pl
from jax.experimental.pallas import tpu as pltpu
from jax.sharding import PartitionSpec as P

MESH = pl.DeviceIdType.MESH
CHUNK = 512
SUB = 16
GROUPS = ((0, 2), (2, 4), (4, 6), (6, 7), (7, 8))
DEPTH = 3
LATE = 3
PLAN = (
    "h0", "h1", "a2", "a3", "m", "d", "t0", "t1", "c0", "c1",
    "h2", "a4", "t2", "h3", "h4", "s", "c2", "t3", "t4", "c3",
    "w", "g0", "g1", "c4", "g2", "g3", "r", "g4",
)


def plain_body(tokens, gate_weight, up_weight, down_weight, right_factor, left_factor):
    fsdp_count = lax.axis_size("fsdp")
    tensor_count = lax.axis_size("tensor")
    tok_local = tokens.shape[0]
    group_rows = tok_local * fsdp_count
    share_rows = group_rows // tensor_count
    hid_local = gate_weight.shape[1]
    spread = lax.all_to_all(tokens, "fsdp", split_axis=1, concat_axis=0, tiled=True)
    student_in = lax.dynamic_slice_in_dim(
        spread, lax.axis_index("tensor") * share_rows, share_rows, 0
    )
    gate_part = jnp.dot(spread, gate_weight, preferred_element_type=jnp.float32)
    up_part = jnp.dot(spread, up_weight, preferred_element_type=jnp.float32)
    partial_value = jnp.concatenate([gate_part, up_part], axis=1)
    summed = lax.psum(partial_value.astype(jnp.bfloat16), "fsdp").astype(jnp.float32)
    hidden = (jax.nn.silu(summed[:, :hid_local]) * summed[:, hid_local:]).astype(jnp.bfloat16)
    target = lax.psum_scatter(
        jnp.dot(hidden, down_weight, preferred_element_type=jnp.float32).astype(jnp.bfloat16),
        "tensor",
        scatter_dimension=0,
        tiled=True,
    ).astype(jnp.float32)
    right_full, left_full = (
        lax.all_gather(right_factor, "tensor", axis=1, tiled=True),
        lax.all_gather(left_factor, "tensor", axis=1, tiled=True),
    )
    blocks_local = right_full.shape[0]
    block_size = right_full.shape[2]
    block_input = student_in.reshape(share_rows, blocks_local, block_size)
    mixed = jnp.einsum(
        "nij,ikj->nik", block_input, right_full, preferred_element_type=jnp.float32
    ).astype(jnp.bfloat16)
    routed = lax.all_to_all(mixed, "fsdp", split_axis=2, concat_axis=1, tiled=True)
    student = jnp.einsum("nij,jki->njk", routed, left_full, preferred_element_type=jnp.float32)
    inv_root = 1.0 / math.sqrt(group_rows)
    out_grad = (student - target.reshape(student.shape)) * inv_root
    grad_left = jnp.einsum("njk,nij->jki", out_grad, routed.astype(jnp.float32))
    mixed_grad = jnp.einsum("njk,jki->nij", out_grad, left_full.astype(jnp.float32)).astype(
        jnp.bfloat16
    )
    returned = lax.all_to_all(mixed_grad, "fsdp", split_axis=1, concat_axis=2, tiled=True)
    grad_right = jnp.einsum(
        "nik,nij->ikj", returned.astype(jnp.float32), block_input.astype(jnp.float32)
    )
    grad_right, grad_left = (
        lax.psum_scatter(grad_right, "tensor", scatter_dimension=1, tiled=True),
        lax.psum_scatter(grad_left, "tensor", scatter_dimension=1, tiled=True),
    )
    return (grad_right, grad_left)


def layer_kernel(
    n, T, width, cols,
    tok, gw, uw, dw, right, left, gr_out, gl_out,
    wg, wu, wd, pbuf, recv_p, recv_x, hid, t_send, t_recv,
    spread, rload, r_s, rki, lji, rbig, lbig, mix_s, routed, mg_s, mg_r, gr_acc, gr_s, gl_acc, gl_s,
    tok_send, tok_recv, tx_send, tx_recv, tf_send, tf_recv, w_sem, d_sem,
    p_send, p_recv, first_send, first_recv, a_send, a_recv, hx_send, hx_recv, hp_send, hp_recv, r_send, r_recv,
    z_send, z_recv, rf_send, rf_recv, lf_send, lf_recv, mix_send, mix_recv, mg_send, mg_recv,
    gr_send, gr_recv, gl_send, gl_recv,
):
    f32, bf16 = jnp.float32, jnp.bfloat16
    f = lax.axis_index("fsdp")
    z = lax.axis_index("tensor")
    x, c = f // 2, f % 2
    partner = x * 2 + (1 - c)
    across = (1 - x) * 2 + c
    diag = (1 - x) * 2 + (1 - c)
    peers = (across, diag, partner)
    parts, rows, features = spread.shape[0], spread.shape[2], spread.shape[3]
    N = parts * 4 * rows
    G = len(GROUPS)
    ni, nk_local, nj = right.shape
    na = nk_local // T
    nk, nb = left.shape[1] * T, left.shape[2]
    nf = na * ni
    iota = functools.partial(lax.broadcasted_iota, jnp.int32)

    def to(peer):
        return dict(device_id={"fsdp": peer}, device_id_type=MESH)

    def along(peer):
        return dict(device_id={"tensor": peer}, device_id_type=MESH)

    def tile(t):
        return pl.ds(pl.multiple_of(t * width, width), width)

    def token_rows(g):
        return slice(GROUPS[g][0] * 4 * rows, GROUPS[g][1] * 4 * rows)

    def weights(t):
        s = lax.rem(t, DEPTH)
        cc = tile(lax.rem(t, n))
        return (
            pltpu.make_async_copy(gw.at[:, cc], wg.at[s], w_sem.at[0, s]),
            pltpu.make_async_copy(uw.at[:, cc], wu.at[s], w_sem.at[1, s]),
        )

    def feature_columns(peer):
        return pl.ds(pl.multiple_of(peer * features, features), features)

    own = pltpu.make_async_copy(
        tok.at[:, :, feature_columns(f)], spread.at[:, f], tok_send.at[0])
    own.start()
    for t in range(DEPTH - 1):
        for cp in weights(t):
            cp.start()
    load_right = pltpu.make_async_copy(right, rload, rf_send.at[0])
    load_right.start()

    barrier = pltpu.get_barrier_semaphore()
    for peer in peers:
        pl.semaphore_signal(barrier, inc=1, **to(peer))
    for d in range(1, T):
        pl.semaphore_signal(barrier, inc=1, **along(lax.rem(z + d, T)))
    load_right.wait()
    wide_right = rload[...].astype(f32)
    for p in range(T):
        r_s[p] = wide_right[:, p * na:(p + 1) * na].reshape(nf, nj).astype(bf16)

    pl.semaphore_wait(barrier, 3 + T - 1)

    half = lax.rem(z, 2)
    z_mate = z + 1 - 2 * half
    span = parts // 4

    def tok_cross(i, j):
        mm = pl.ds(half * (parts // 2) + j * span, span)
        return pltpu.make_async_remote_copy(
            tok.at[mm, :, feature_columns(peers[i])], spread.at[mm, f],
            tx_send.at[i, j], tx_recv.at[i, j], **to(peers[i]))

    def tok_pass(i, j):
        mm = pl.ds(half * (parts // 2) + j * span, span)
        return pltpu.make_async_remote_copy(
            spread.at[mm, peers[i]], spread.at[mm, peers[i]],
            tf_send.at[i, j], tf_recv.at[i, j], **along(z_mate))

    tok_near = pltpu.make_async_remote_copy(
        tok.at[:, :, feature_columns(partner)], spread.at[:, f],
        tok_send.at[1], tok_recv.at[1], **to(partner))
    tok_near.start()
    pieces = [(i, j) for j in range(2) for i in range(2)]
    for i, j in pieces:
        tok_cross(i, j).start()

    def right_copy(d):
        peer = lax.rem(z + d, T)
        return pltpu.make_async_remote_copy(
            r_s.at[peer], rki.at[z], rf_send.at[d], rf_recv.at[d], **along(peer))

    def left_copy(d):
        peer = lax.rem(z + d, T)
        return pltpu.make_async_remote_copy(
            left.at[pl.ds(peer * na, na)], lji.at[:, z], lf_send.at[d], lf_recv.at[d],
            **along(peer))

    factors = [right_copy(d) for d in range(1, T)] + [left_copy(d) for d in range(1, T)]
    for cp in factors:
        cp.start()
    own_left = pltpu.make_async_copy(left.at[pl.ds(z * na, na)], lji.at[:, z], lf_send.at[0])
    own_left.start()
    rki[z] = r_s[z]

    def pair_copy(p, t):
        cc = tile(t)
        return pltpu.make_async_remote_copy(
            pbuf.at[p, 1 - c, :, :, :, cc], recv_p.at[p, :, :, :, cc],
            p_send.at[p, t], p_recv.at[p, t], **to(partner))

    def send_first(t):
        mm = slice(*GROUPS[0])
        cc = tile(t)
        return pltpu.make_async_remote_copy(
            pbuf.at[0, c, mm, :, :, cc], recv_x.at[mm, :, :, cc],
            first_send.at[t], first_recv.at[t], **to(across))

    def pair_sum(p, t):
        pair_copy(p, t).wait_recv()
        cc = tile(t)
        for k in range(2):
            total = pbuf[p, c, :, k, :, cc].astype(f32) + recv_p[p, :, k, :, cc].astype(f32)
            pbuf[p, c, :, k, :, cc] = total.astype(bf16)
        if p == 0:
            send_first(t).start()

    def products(p, t):
        chip = x if p == 0 else 1 - x
        step = p * n + t

        @pl.when(step + DEPTH - 1 < 2 * n)
        def _():
            for cp in weights(step + DEPTH - 1):
                cp.start()

        for cp in weights(step):
            cp.wait()
        s = lax.rem(step, DEPTH)
        toks = spread[:, pl.ds(2 * chip, 2)].reshape(parts * 2 * rows, features)
        cc = tile(t)
        for k, w in ((0, wg), (1, wu)):
            part = jnp.dot(toks, w[s], preferred_element_type=f32).astype(bf16)
            part = part.reshape(parts, 2, rows, width)
            for h in range(2):
                pbuf[p, h, :, k, :, cc] = part[:, h]
        pair_copy(p, t).start()

        @pl.when(t >= 1)
        def _():
            pair_sum(p, t - 1)

    own.wait()
    tok_near.wait_recv()

    def first_half(t, carry):
        products(0, t)
        for q, (i, j) in enumerate(pieces):
            @pl.when(t == 2 * q + 1)
            def _():
                tok_cross(i, j).wait_recv()
                tok_pass(i, j).start()
        return carry

    lax.fori_loop(0, n, first_half, 0)
    pair_sum(0, n - 1)

    def send_a(g):
        mm = slice(*GROUPS[g])
        return pltpu.make_async_remote_copy(
            pbuf.at[0, c, mm], recv_x.at[mm], a_send.at[g], a_recv.at[g], **to(across))

    send_a(1).start()
    for q, (i, j) in enumerate(pieces):
        if 2 * q + 1 >= n:
            tok_cross(i, j).wait_recv()
            tok_pass(i, j).start()

    own_left.wait()
    for cp in factors:
        cp.wait()
    packed = rki[...].reshape(T * nf, nj)
    lane_block = lax.rem(iota((T * nf, nj), 0), nf) // na
    for i in range(ni):
        rbig[:, i * nj:(i + 1) * nj] = jnp.where(lane_block == i, packed, jnp.zeros_like(packed))
    col = lax.rem(iota((nb, 4 * nf), 1), nf)
    pick = iota((nb, 4 * nf), 0) == (iota((nb, 4 * nf), 1) // nf) * ni + col // na
    wide = jnp.dot(
        lji[...].reshape(na * nk, nb), pick.astype(f32).astype(bf16), preferred_element_type=f32)
    same = iota((na * nk, 4 * nf), 0) // nk == lax.rem(iota((na * nk, 4 * nf), 1), na)
    lbig[...] = jnp.where(same, wide, 0.0).astype(bf16)

    for i, j in pieces:
        tok_pass(i, j).wait_recv()

    def second_half(t, carry):
        products(1, t)
        return carry

    lax.fori_loop(0, n, second_half, 0)
    load_down = pltpu.make_async_copy(dw, wd, d_sem)
    load_down.start()
    pair_sum(1, n - 1)

    mine = pl.ds(pl.multiple_of(f * nf, nf), nf)

    def mix_copy(i):
        return pltpu.make_async_remote_copy(
            mix_s.at[:, pl.ds(pl.multiple_of(peers[i] * nf, nf), nf)],
            routed.at[:, pl.ds(pl.multiple_of(f * nf, nf), nf)],
            mix_send.at[i], mix_recv.at[i], **to(peers[i]))

    def send_hx(g):
        mm = slice(*GROUPS[g])
        return pltpu.make_async_remote_copy(
            hid.at[mm, across], hid.at[mm, across], hx_send.at[g], hx_recv.at[g], **to(across))

    def send_hp(g):
        mm = slice(*GROUPS[g])
        return pltpu.make_async_remote_copy(
            hid.at[mm, across], hid.at[mm, across], hp_send.at[g], hp_recv.at[g], **to(partner))

    def send_r(g):
        mm = slice(*GROUPS[g])
        return pltpu.make_async_remote_copy(
            hid.at[mm, f], hid.at[mm, f], r_send.at[g], r_recv.at[g], **to(partner))

    side = z // 2
    far = 2 * (1 - side)
    inner = (z == 1) | (z == 2)

    def z_near(g, i):
        rr = token_rows(g)
        b = z_mate if i is None else far + i
        k = 0 if i is None else 1 + i
        return pltpu.make_async_remote_copy(
            t_send.at[b, rr], t_recv.at[k, rr], z_send.at[g, k], z_recv.at[g, k],
            **along(z_mate))

    def z_far(g, i):
        rr = token_rows(g)
        return pltpu.make_async_remote_copy(
            t_send.at[far + i, rr], t_recv.at[3, rr], z_send.at[g, 1 + i], z_recv.at[g, 3],
            **along(far + i))

    def mg_copy(g, i):
        rr = token_rows(g)
        return pltpu.make_async_remote_copy(
            mg_s.at[rr, pl.ds(pl.multiple_of(peers[i] * nf, nf), nf)], mg_r.at[f, rr],
            mg_send.at[g, i], mg_recv.at[g, i], **to(peers[i]))

    def make_hidden(g):
        mm = slice(*GROUPS[g])
        if g > 0:
            send_a(g).wait_recv()

        @pl.loop(0, n)
        def _(t):
            if g == 0:
                send_first(t).wait_recv()
            cc = tile(t)
            gate = pbuf[1, c, mm, 0, :, cc].astype(f32) + recv_x[mm, 0, :, cc].astype(f32)
            up = pbuf[1, c, mm, 1, :, cc].astype(f32) + recv_x[mm, 1, :, cc].astype(f32)
            hid[mm, across, :, cc] = (jax.nn.silu(gate) * up).astype(bf16)

        send_hx(g).start()
        send_hp(g).start()

    def make_target(g):
        m0, m1 = GROUPS[g]
        rr = token_rows(g)
        send_hx(g).wait_recv()
        send_r(g).start()
        send_hp(g).wait_recv()
        send_r(g).wait_recv()

        @pl.loop(0, T)
        def _(i):
            b = 2 * lax.rem(side + 1 + i // 2, 2) + lax.rem(i + (i // 2) * (z + 1), 2)
            cc = pl.ds(pl.multiple_of(b * cols, cols), cols)
            h = hid[m0:m1].reshape((m1 - m0) * 4 * rows, n * width)
            t_send[b, rr] = jnp.dot(h, wd[:, cc], preferred_element_type=f32).astype(bf16)

            for k in range(2):
                @pl.when((i == k) & jnp.logical_not(inner))
                def _():
                    z_near(g, k).start()

            @pl.when(i == 2)
            def _():
                z_near(g, None).start()

    def combine(g):
        rr = token_rows(g)

        @pl.when(inner)
        def _():
            for k in range(2):
                z_near(g, k).wait_recv()
                total = t_send[far + k, rr].astype(f32) + t_recv[1 + k, rr].astype(f32)
                t_send[far + k, rr] = total.astype(bf16)
                z_far(g, k).start()

    def make_grads(g, first):
        rr = token_rows(g)
        student = lax.dot_general(
            routed[rr], lbig[...], (((1,), (1,)), ((), ())), preferred_element_type=f32)
        z_near(g, None).wait_recv()
        z_far(g, 0).wait_recv()
        tgt = t_send[z, rr].astype(f32) + t_recv[0, rr].astype(f32) + t_recv[3, rr].astype(f32)
        out_grad = (student - tgt) * (1.0 / math.sqrt(N))
        mg_s[rr] = jnp.dot(
            out_grad.astype(bf16), lbig[...], preferred_element_type=f32).astype(bf16)
        for i in range(3):
            mg_copy(g, i).start()
        mg_r[f, rr] = mg_s[rr, mine]
        part = jnp.dot(out_grad.T.astype(bf16), routed[rr], preferred_element_type=f32)
        if first:
            gl_acc[...] = part
        else:
            gl_acc[...] += part

    row_block = iota((nf, nj), 0) // na

    def right_terms(b, m0, m1):
        rr = slice(m0 * 4 * rows, m1 * 4 * rows)
        flipped = mg_r[b, rr].astype(f32).T.astype(bf16)
        total = jnp.zeros((nf, nj), f32)
        for i in range(0, ni, 2):
            rhs = spread[m0:m1, :, :, i * nj:(i + 2) * nj].reshape((m1 - m0) * 4 * rows, 2 * nj)
            part = jnp.dot(flipped, rhs, preferred_element_type=f32)
            for k in range(2):
                total += jnp.where(row_block == i + k, part[:, k * nj:(k + 1) * nj], 0.0)
        return total

    def make_mixed():
        mix_s[...] = lax.dot_general(
            spread[...].reshape(N, features), rbig[...], (((1,), (1,)), ((), ())),
            preferred_element_type=f32).astype(bf16)
        routed[:, mine] = mix_s[:, mine]

    def send_mixed():
        for i in range(3):
            mix_copy(i).start()

    def wait_mixed():
        for i in range(3):
            mix_copy(i).wait_recv()

    early = GROUPS[LATE][0]

    def early_right():
        for g in range(LATE):
            for i in range(3):
                mg_copy(g, i).wait_recv()

        @pl.loop(0, 4)
        def _(b):
            gr_acc[b] = right_terms(b, 0, early)

    stages = {
        "a": lambda g: send_a(g).start(),
        "h": make_hidden,
        "m": lambda g: make_mixed(),
        "s": lambda g: send_mixed(),
        "w": lambda g: wait_mixed(),
        "d": lambda g: load_down.wait(),
        "t": make_target,
        "c": combine,
        "g": lambda g: make_grads(g, g == 0),
        "r": lambda g: early_right(),
    }
    for step in PLAN:
        stages[step[0]](int(step[1:] or 0))

    def gl_copy(d):
        peer = lax.rem(z + d, T)
        return pltpu.make_async_remote_copy(
            gl_s.at[:, peer], gl_out.at[pl.ds(z * na, na)], gl_send.at[d], gl_recv.at[d],
            **along(peer))

    def gr_copy(b):
        return pltpu.make_async_remote_copy(
            gr_s.at[b], gr_out.at[z], gr_send.at[b], gr_recv.at[z], **along(b))

    shape = (na * nk, 4 * nf)
    keep = iota(shape, 0) // nk == lax.rem(iota(shape, 1), na)
    fold = iota((4 * nf, nb), 1) == (iota((4 * nf, nb), 0) // nf) * ni + lax.rem(
        iota((4 * nf, nb), 0), nf) // na
    total = jnp.dot(
        jnp.where(keep, gl_acc[...], 0.0).astype(bf16), fold.astype(f32).astype(bf16),
        preferred_element_type=f32)
    gl_s[...] = total.astype(bf16).reshape(na, T, nk // T, nb)
    for d in range(1, T):
        gl_copy(d).start()
    gl_out[pl.ds(z * na, na)] = gl_s[:, z]

    def finish_right(b):
        gr_s[b] = (gr_acc[b] + right_terms(b, early, parts)).astype(bf16)

        @pl.when(b != z)
        def _():
            gr_copy(b).start()

        @pl.when(b == z)
        def _():
            gr_out[z] = gr_s[b]

    finish_right(f)
    for i in (2, 0, 1):
        for g in range(LATE, G):
            mg_copy(g, i).wait_recv()
        finish_right(peers[i])

    for d in range(1, T):
        gl_copy(d).wait()
    for b in range(T):
        @pl.when(z != b)
        def _():
            gr_copy(b).wait_send()
            pltpu.make_async_remote_copy(
                gr_s.at[b], gr_out.at[b], gr_send.at[b], gr_recv.at[b], **along(b)).wait_recv()

    tok_near.wait_send()
    for i, j in pieces:
        tok_cross(i, j).wait_send()
        tok_pass(i, j).wait_send()
    for i in range(3):
        mix_copy(i).wait_send()
    for g in range(G):
        if g > 0:
            send_a(g).wait_send()
        for cp in (send_hx(g), send_hp(g), send_r(g)):
            cp.wait_send()
        z_near(g, None).wait_send()
        for k in range(2):
            @pl.when(inner)
            def _():
                z_far(g, k).wait_send()

            @pl.when(jnp.logical_not(inner))
            def _():
                z_near(g, k).wait_send()

        for i in range(3):
            mg_copy(g, i).wait_send()

    def drain(t, carry):
        for p in range(2):
            pair_copy(p, t).wait_send()
        send_first(t).wait_send()
        return carry

    lax.fori_loop(0, n, drain, 0)


def fused_body(tokens, gate_weight, up_weight, down_weight, right_factor, left_factor):
    T = lax.axis_size("tensor")
    rows = SUB
    parts = tokens.shape[0] // rows
    tok = tokens.reshape(parts, rows, tokens.shape[1])
    features, hidden = gate_weight.shape
    width = CHUNK
    n = hidden // width
    G = len(GROUPS)
    cols = down_weight.shape[1] // T
    bf16, f32 = jnp.bfloat16, jnp.float32
    dma = pltpu.SemaphoreType.DMA
    anyspace = pl.BlockSpec(memory_space=pl.ANY)
    vmem = pl.BlockSpec(memory_space=pltpu.VMEM)
    ni, nkr, nj = right_factor.shape
    na, nkl, nb = left_factor.shape[0] // T, left_factor.shape[1], left_factor.shape[2]
    nf, nk = na * ni, nkl * T
    N = 4 * parts * rows
    right_parts, left_parts = pl.pallas_call(
        functools.partial(layer_kernel, n, T, width, cols),
        out_shape=(
            jax.ShapeDtypeStruct((T, nf, nj), bf16),
            jax.ShapeDtypeStruct((T * na, nkl, nb), bf16),
        ),
        in_specs=[anyspace] * 6,
        out_specs=(vmem, vmem),
        scratch_shapes=[
            pltpu.VMEM((DEPTH, features, width), bf16),
            pltpu.VMEM((DEPTH, features, width), bf16),
            pltpu.VMEM((hidden, T * cols), bf16),
            pltpu.VMEM((2, 2, parts, 2, rows, hidden), bf16),
            pltpu.VMEM((2, parts, 2, rows, hidden), bf16),
            pltpu.VMEM((parts, 2, rows, hidden), bf16),
            pltpu.VMEM((parts, 4, rows, hidden), bf16),
            pltpu.VMEM((T, N, cols), bf16),
            pltpu.VMEM((4, N, cols), bf16),
            pltpu.VMEM((parts, 4, rows, features), bf16),
            pltpu.VMEM((ni, nkr, nj), bf16),
            pltpu.VMEM((T, nf, nj), bf16),
            pltpu.VMEM((T, nf, nj), bf16),
            pltpu.VMEM((na, T, nkl, nb), bf16),
            pltpu.VMEM((4 * nf, features), bf16),
            pltpu.VMEM((na * nk, 4 * nf), bf16),
            pltpu.VMEM((N, 4 * nf), bf16),
            pltpu.VMEM((N, 4 * nf), bf16),
            pltpu.VMEM((N, 4 * nf), bf16),
            pltpu.VMEM((4, N, nf), bf16),
            pltpu.VMEM((4, nf, nj), f32),
            pltpu.VMEM((4, nf, nj), bf16),
            pltpu.VMEM((na * nk, 4 * nf), f32),
            pltpu.VMEM((na, T, nkl, nb), bf16),
            dma((2,)), dma((2,)), dma((2, 2)), dma((2, 2)), dma((2, 2)), dma((2, 2)),
            dma((2, DEPTH)), dma,
            dma((2, n)), dma((2, n)), dma((n,)), dma((n,)), dma((G,)), dma((G,)),
            dma((G,)), dma((G,)), dma((G,)), dma((G,)), dma((G,)), dma((G,)),
            dma((G, 3)), dma((G, 4)),
            dma((T,)), dma((T,)), dma((T,)), dma((T,)),
            dma((3,)), dma((3,)), dma((G, 3)), dma((G, 3)),
            dma((T,)), dma((T,)), dma((T,)), dma((T,)),
        ],
        compiler_params=pltpu.CompilerParams(
            collective_id=0, has_side_effects=True, vmem_limit_bytes=62 * 1024 * 1024
        ),
        name="layer",
    )(tok, gate_weight, up_weight, down_weight, right_factor, left_factor)

    def widen(right_ref, left_ref, right_out, left_out):
        for t in range(T):
            right_out[:, t * na:(t + 1) * na] = right_ref[t].astype(f32).reshape(ni, na, nj)
        left_out[...] = left_ref[...].astype(f32)

    return pl.pallas_call(
        widen,
        out_shape=(
            jax.ShapeDtypeStruct((ni, nkr, nj), f32),
            jax.ShapeDtypeStruct((T * na, nkl, nb), f32),
        ),
        in_specs=[vmem] * 2,
        out_specs=(vmem, vmem),
        name="widen",
    )(right_parts, left_parts)


def body(tokens, gate_weight, up_weight, down_weight, right_factor, left_factor):
    F, T = lax.axis_size("fsdp"), lax.axis_size("tensor")
    fits = (
        F == 4
        and T == 4
        and gate_weight.shape[1] % CHUNK == 0
        and left_factor.shape[0] % T == 0
        and right_factor.shape[1] % T == 0
        and gate_weight.shape[0] <= 2048
        and tokens.shape[0] == 128
    )
    run = fused_body if fits else plain_body
    return run(tokens, gate_weight, up_weight, down_weight, right_factor, left_factor)


def solution(mesh):
    return jax.shard_map(
        body,
        mesh=mesh,
        in_specs=(
            P(("groups", "fsdp"), None),
            P("fsdp", "tensor"),
            P("fsdp", "tensor"),
            P("tensor", "fsdp"),
            P("fsdp", "tensor", None),
            P("fsdp", "tensor", None),
        ),
        out_specs=(P(("groups", "fsdp"), "tensor", None), P(("groups", "fsdp"), "tensor", None)),
        check_vma=False,
    )
```

```python
import functools
import math

import jax
import jax.numpy as jnp
from jax import lax
from jax.experimental import pallas as pl
from jax.experimental.pallas import tpu as pltpu
from jax.sharding import PartitionSpec as P

MESH = pl.DeviceIdType.MESH
CHUNK = 512
SUB = 16
GROUPS = ((0, 2), (2, 4), (4, 6), (6, 7), (7, 8))
DEPTH = 3
LATE = 2
PLAN = (
    "h0", "h1", "a2", "a3", "m", "d", "t0", "t1", "c0", "h2",
    "a4", "c1", "t2", "h3", "h4", "s", "t3", "c2", "t4", "c3",
    "w", "g0", "g1", "c4", "g2", "r", "g3", "g4",
)


def plain_body(tokens, gate_weight, up_weight, down_weight, right_factor, left_factor):
    fsdp_count = lax.axis_size("fsdp")
    tensor_count = lax.axis_size("tensor")
    tok_local = tokens.shape[0]
    group_rows = tok_local * fsdp_count
    share_rows = group_rows // tensor_count
    hid_local = gate_weight.shape[1]
    spread = lax.all_to_all(tokens, "fsdp", split_axis=1, concat_axis=0, tiled=True)
    student_in = lax.dynamic_slice_in_dim(
        spread, lax.axis_index("tensor") * share_rows, share_rows, 0
    )
    gate_part = jnp.dot(spread, gate_weight, preferred_element_type=jnp.float32)
    up_part = jnp.dot(spread, up_weight, preferred_element_type=jnp.float32)
    partial_value = jnp.concatenate([gate_part, up_part], axis=1)
    summed = lax.psum(partial_value.astype(jnp.bfloat16), "fsdp").astype(jnp.float32)
    hidden = (jax.nn.silu(summed[:, :hid_local]) * summed[:, hid_local:]).astype(jnp.bfloat16)
    target = lax.psum_scatter(
        jnp.dot(hidden, down_weight, preferred_element_type=jnp.float32).astype(jnp.bfloat16),
        "tensor",
        scatter_dimension=0,
        tiled=True,
    ).astype(jnp.float32)
    right_full, left_full = (
        lax.all_gather(right_factor, "tensor", axis=1, tiled=True),
        lax.all_gather(left_factor, "tensor", axis=1, tiled=True),
    )
    blocks_local = right_full.shape[0]
    block_size = right_full.shape[2]
    block_input = student_in.reshape(share_rows, blocks_local, block_size)
    mixed = jnp.einsum(
        "nij,ikj->nik", block_input, right_full, preferred_element_type=jnp.float32
    ).astype(jnp.bfloat16)
    routed = lax.all_to_all(mixed, "fsdp", split_axis=2, concat_axis=1, tiled=True)
    student = jnp.einsum("nij,jki->njk", routed, left_full, preferred_element_type=jnp.float32)
    inv_root = 1.0 / math.sqrt(group_rows)
    out_grad = (student - target.reshape(student.shape)) * inv_root
    grad_left = jnp.einsum("njk,nij->jki", out_grad, routed.astype(jnp.float32))
    mixed_grad = jnp.einsum("njk,jki->nij", out_grad, left_full.astype(jnp.float32)).astype(
        jnp.bfloat16
    )
    returned = lax.all_to_all(mixed_grad, "fsdp", split_axis=1, concat_axis=2, tiled=True)
    grad_right = jnp.einsum(
        "nik,nij->ikj", returned.astype(jnp.float32), block_input.astype(jnp.float32)
    )
    grad_right, grad_left = (
        lax.psum_scatter(grad_right, "tensor", scatter_dimension=1, tiled=True),
        lax.psum_scatter(grad_left, "tensor", scatter_dimension=1, tiled=True),
    )
    return (grad_right, grad_left)


def layer_kernel(
    n, T, width, cols,
    tok, gw, uw, dw, right, left, gr_out, gl_out,
    wg, wu, wd, pbuf, recv_p, recv_x, hid, t_send, t_recv,
    spread, rload, r_s, rki, lji, rbig, lbig, mix_s, routed, mg_s, mg_r, gr_acc, gr_s, gl_acc, gl_s,
    tok_send, tok_recv, tx_send, tx_recv, tf_send, tf_recv, w_sem, d_sem,
    p_send, p_recv, first_send, first_recv, a_send, a_recv, hx_send, hx_recv, hp_send, hp_recv, r_send, r_recv,
    z_send, z_recv, rf_send, rf_recv, lf_send, lf_recv, mix_send, mix_recv, mg_send, mg_recv,
    gr_send, gr_recv, gl_send, gl_recv,
):
    f32, bf16 = jnp.float32, jnp.bfloat16
    f = lax.axis_index("fsdp")
    z = lax.axis_index("tensor")
    x, c = f // 2, f % 2
    partner = x * 2 + (1 - c)
    across = (1 - x) * 2 + c
    diag = (1 - x) * 2 + (1 - c)
    peers = (across, diag, partner)
    parts, rows, features = spread.shape[0], spread.shape[2], spread.shape[3]
    N = parts * 4 * rows
    G = len(GROUPS)
    ni, nk_local, nj = right.shape
    na = nk_local // T
    nk, nb = left.shape[1] * T, left.shape[2]
    nf = na * ni
    iota = functools.partial(lax.broadcasted_iota, jnp.int32)

    def to(peer):
        return dict(device_id={"fsdp": peer}, device_id_type=MESH)

    def along(peer):
        return dict(device_id={"tensor": peer}, device_id_type=MESH)

    def tile(t):
        return pl.ds(pl.multiple_of(t * width, width), width)

    def token_rows(g):
        return slice(GROUPS[g][0] * 4 * rows, GROUPS[g][1] * 4 * rows)

    def weights(t):
        s = lax.rem(t, DEPTH)
        cc = tile(lax.rem(t, n))
        return (
            pltpu.make_async_copy(gw.at[:, cc], wg.at[s], w_sem.at[0, s]),
            pltpu.make_async_copy(uw.at[:, cc], wu.at[s], w_sem.at[1, s]),
        )

    def feature_columns(peer):
        return pl.ds(pl.multiple_of(peer * features, features), features)

    own = pltpu.make_async_copy(
        tok.at[:, :, feature_columns(f)], spread.at[:, f], tok_send.at[0])
    own.start()
    for t in range(DEPTH - 1):
        for cp in weights(t):
            cp.start()
    load_right = pltpu.make_async_copy(right, rload, rf_send.at[0])
    load_right.start()

    barrier = pltpu.get_barrier_semaphore()
    for peer in peers:
        pl.semaphore_signal(barrier, inc=1, **to(peer))
    for d in range(1, T):
        pl.semaphore_signal(barrier, inc=1, **along(lax.rem(z + d, T)))
    load_right.wait()
    wide_right = rload[...].astype(f32)
    for p in range(T):
        r_s[p] = wide_right[:, p * na:(p + 1) * na].reshape(nf, nj).astype(bf16)

    pl.semaphore_wait(barrier, 3 + T - 1)

    half = lax.rem(z, 2)
    z_mate = z + 1 - 2 * half
    span = parts // 4

    def tok_cross(i, j):
        mm = pl.ds(half * (parts // 2) + j * span, span)
        return pltpu.make_async_remote_copy(
            tok.at[mm, :, feature_columns(peers[i])], spread.at[mm, f],
            tx_send.at[i, j], tx_recv.at[i, j], **to(peers[i]))

    def tok_pass(i, j):
        mm = pl.ds(half * (parts // 2) + j * span, span)
        return pltpu.make_async_remote_copy(
            spread.at[mm, peers[i]], spread.at[mm, peers[i]],
            tf_send.at[i, j], tf_recv.at[i, j], **along(z_mate))

    tok_near = pltpu.make_async_remote_copy(
        tok.at[:, :, feature_columns(partner)], spread.at[:, f],
        tok_send.at[1], tok_recv.at[1], **to(partner))
    tok_near.start()
    pieces = [(i, j) for j in range(2) for i in range(2)]
    for i, j in pieces:
        tok_cross(i, j).start()

    def right_copy(d):
        peer = lax.rem(z + d, T)
        return pltpu.make_async_remote_copy(
            r_s.at[peer], rki.at[z], rf_send.at[d], rf_recv.at[d], **along(peer))

    def left_copy(d):
        peer = lax.rem(z + d, T)
        return pltpu.make_async_remote_copy(
            left.at[pl.ds(peer * na, na)], lji.at[:, z], lf_send.at[d], lf_recv.at[d],
            **along(peer))

    factors = [right_copy(d) for d in range(1, T)] + [left_copy(d) for d in range(1, T)]
    for cp in factors:
        cp.start()
    own_left = pltpu.make_async_copy(left.at[pl.ds(z * na, na)], lji.at[:, z], lf_send.at[0])
    own_left.start()
    rki[z] = r_s[z]

    def pair_copy(p, t):
        cc = tile(t)
        return pltpu.make_async_remote_copy(
            pbuf.at[p, 1 - c, :, :, :, cc], recv_p.at[p, :, :, :, cc],
            p_send.at[p, t], p_recv.at[p, t], **to(partner))

    def send_first(t):
        mm = slice(*GROUPS[0])
        cc = tile(t)
        return pltpu.make_async_remote_copy(
            pbuf.at[0, c, mm, :, :, cc], recv_x.at[mm, :, :, cc],
            first_send.at[t], first_recv.at[t], **to(across))

    def pair_sum(p, t):
        pair_copy(p, t).wait_recv()
        cc = tile(t)
        for k in range(2):
            total = pbuf[p, c, :, k, :, cc].astype(f32) + recv_p[p, :, k, :, cc].astype(f32)
            pbuf[p, c, :, k, :, cc] = total.astype(bf16)
        if p == 0:
            send_first(t).start()

    def products(p, t):
        chip = x if p == 0 else 1 - x
        step = p * n + t

        @pl.when(step + DEPTH - 1 < 2 * n)
        def _():
            for cp in weights(step + DEPTH - 1):
                cp.start()

        for cp in weights(step):
            cp.wait()
        s = lax.rem(step, DEPTH)
        toks = spread[:, pl.ds(2 * chip, 2)].reshape(parts * 2 * rows, features)
        cc = tile(t)
        for k, w in ((0, wg), (1, wu)):
            part = jnp.dot(toks, w[s], preferred_element_type=f32).astype(bf16)
            part = part.reshape(parts, 2, rows, width)
            for h in range(2):
                pbuf[p, h, :, k, :, cc] = part[:, h]
        pair_copy(p, t).start()

        @pl.when(t >= 1)
        def _():
            pair_sum(p, t - 1)

    own.wait()
    tok_near.wait_recv()

    def first_half(t, carry):
        products(0, t)
        for q, (i, j) in enumerate(pieces):
            @pl.when(t == 2 * q + 1)
            def _():
                tok_cross(i, j).wait_recv()
                tok_pass(i, j).start()
        return carry

    lax.fori_loop(0, n, first_half, 0)
    pair_sum(0, n - 1)

    def send_a(g):
        mm = slice(*GROUPS[g])
        return pltpu.make_async_remote_copy(
            pbuf.at[0, c, mm], recv_x.at[mm], a_send.at[g], a_recv.at[g], **to(across))

    send_a(1).start()
    for q, (i, j) in enumerate(pieces):
        if 2 * q + 1 >= n:
            tok_cross(i, j).wait_recv()
            tok_pass(i, j).start()

    own_left.wait()
    for cp in factors:
        cp.wait()
    packed = rki[...].reshape(T * nf, nj)
    lane_block = lax.rem(iota((T * nf, nj), 0), nf) // na
    for i in range(ni):
        rbig[:, i * nj:(i + 1) * nj] = jnp.where(lane_block == i, packed, jnp.zeros_like(packed))
    col = lax.rem(iota((nb, 4 * nf), 1), nf)
    pick = iota((nb, 4 * nf), 0) == (iota((nb, 4 * nf), 1) // nf) * ni + col // na
    wide = jnp.dot(
        lji[...].reshape(na * nk, nb), pick.astype(f32).astype(bf16), preferred_element_type=f32)
    same = iota((na * nk, 4 * nf), 0) // nk == lax.rem(iota((na * nk, 4 * nf), 1), na)
    lbig[...] = jnp.where(same, wide, 0.0).astype(bf16)

    for i, j in pieces:
        tok_pass(i, j).wait_recv()

    def second_half(t, carry):
        products(1, t)
        return carry

    lax.fori_loop(0, n, second_half, 0)
    load_down = pltpu.make_async_copy(dw, wd, d_sem)
    load_down.start()
    pair_sum(1, n - 1)

    mine = pl.ds(pl.multiple_of(f * nf, nf), nf)

    def mix_copy(i):
        return pltpu.make_async_remote_copy(
            mix_s.at[:, pl.ds(pl.multiple_of(peers[i] * nf, nf), nf)],
            routed.at[:, pl.ds(pl.multiple_of(f * nf, nf), nf)],
            mix_send.at[i], mix_recv.at[i], **to(peers[i]))

    def send_hx(g):
        mm = slice(*GROUPS[g])
        return pltpu.make_async_remote_copy(
            hid.at[mm, across], hid.at[mm, across], hx_send.at[g], hx_recv.at[g], **to(across))

    def send_hp(g):
        mm = slice(*GROUPS[g])
        return pltpu.make_async_remote_copy(
            hid.at[mm, across], hid.at[mm, across], hp_send.at[g], hp_recv.at[g], **to(partner))

    def send_r(g):
        mm = slice(*GROUPS[g])
        return pltpu.make_async_remote_copy(
            hid.at[mm, f], hid.at[mm, f], r_send.at[g], r_recv.at[g], **to(partner))

    side = z // 2
    far = 2 * (1 - side)
    inner = (z == 1) | (z == 2)

    def z_near(g, i):
        rr = token_rows(g)
        b = z_mate if i is None else far + i
        k = 0 if i is None else 1 + i
        return pltpu.make_async_remote_copy(
            t_send.at[b, rr], t_recv.at[k, rr], z_send.at[g, k], z_recv.at[g, k],
            **along(z_mate))

    def z_far(g, i):
        rr = token_rows(g)
        return pltpu.make_async_remote_copy(
            t_send.at[far + i, rr], t_recv.at[3, rr], z_send.at[g, 1 + i], z_recv.at[g, 3],
            **along(far + i))

    def mg_copy(g, i):
        rr = token_rows(g)
        return pltpu.make_async_remote_copy(
            mg_s.at[rr, pl.ds(pl.multiple_of(peers[i] * nf, nf), nf)], mg_r.at[f, rr],
            mg_send.at[g, i], mg_recv.at[g, i], **to(peers[i]))

    def make_hidden(g):
        mm = slice(*GROUPS[g])
        if g > 0:
            send_a(g).wait_recv()

        @pl.loop(0, n)
        def _(t):
            if g == 0:
                send_first(t).wait_recv()
            cc = tile(t)
            gate = pbuf[1, c, mm, 0, :, cc].astype(f32) + recv_x[mm, 0, :, cc].astype(f32)
            up = pbuf[1, c, mm, 1, :, cc].astype(f32) + recv_x[mm, 1, :, cc].astype(f32)
            hid[mm, across, :, cc] = (jax.nn.silu(gate) * up).astype(bf16)

        send_hx(g).start()
        send_hp(g).start()

    def make_target(g):
        m0, m1 = GROUPS[g]
        rr = token_rows(g)
        send_hx(g).wait_recv()
        send_r(g).start()
        send_hp(g).wait_recv()
        send_r(g).wait_recv()

        @pl.loop(0, T)
        def _(i):
            b = 2 * lax.rem(side + 1 + i // 2, 2) + lax.rem(i + (i // 2) * (z + 1), 2)
            cc = pl.ds(pl.multiple_of(b * cols, cols), cols)
            h = hid[m0:m1].reshape((m1 - m0) * 4 * rows, n * width)
            t_send[b, rr] = jnp.dot(h, wd[:, cc], preferred_element_type=f32).astype(bf16)

            for k in range(2):
                @pl.when((i == k) & jnp.logical_not(inner))
                def _():
                    z_near(g, k).start()

            @pl.when(i == 2)
            def _():
                z_near(g, None).start()

    def combine(g):
        rr = token_rows(g)

        @pl.when(inner)
        def _():
            for k in range(2):
                z_near(g, k).wait_recv()
                total = t_send[far + k, rr].astype(f32) + t_recv[1 + k, rr].astype(f32)
                t_send[far + k, rr] = total.astype(bf16)
                z_far(g, k).start()

    def make_grads(g, first):
        rr = token_rows(g)
        student = lax.dot_general(
            routed[rr], lbig[...], (((1,), (1,)), ((), ())), preferred_element_type=f32)
        z_near(g, None).wait_recv()
        z_far(g, 0).wait_recv()
        tgt = t_send[z, rr].astype(f32) + t_recv[0, rr].astype(f32) + t_recv[3, rr].astype(f32)
        out_grad = (student - tgt) * (1.0 / math.sqrt(N))
        mg_s[rr] = jnp.dot(
            out_grad.astype(bf16), lbig[...], preferred_element_type=f32).astype(bf16)
        for i in range(3):
            mg_copy(g, i).start()
        mg_r[f, rr] = mg_s[rr, mine]
        part = jnp.dot(out_grad.T.astype(bf16), routed[rr], preferred_element_type=f32)
        if first:
            gl_acc[...] = part
        else:
            gl_acc[...] += part

    row_block = iota((nf, nj), 0) // na

    def right_terms(b, m0, m1):
        rr = slice(m0 * 4 * rows, m1 * 4 * rows)
        flipped = mg_r[b, rr].astype(f32).T.astype(bf16)
        total = jnp.zeros((nf, nj), f32)
        for i in range(0, ni, 2):
            rhs = spread[m0:m1, :, :, i * nj:(i + 2) * nj].reshape((m1 - m0) * 4 * rows, 2 * nj)
            part = jnp.dot(flipped, rhs, preferred_element_type=f32)
            for k in range(2):
                total += jnp.where(row_block == i + k, part[:, k * nj:(k + 1) * nj], 0.0)
        return total

    def make_mixed():
        mix_s[...] = lax.dot_general(
            spread[...].reshape(N, features), rbig[...], (((1,), (1,)), ((), ())),
            preferred_element_type=f32).astype(bf16)
        routed[:, mine] = mix_s[:, mine]

    def send_mixed():
        for i in range(3):
            mix_copy(i).start()

    def wait_mixed():
        for i in range(3):
            mix_copy(i).wait_recv()

    early = GROUPS[LATE][0]

    def early_right():
        for g in range(LATE):
            for i in range(3):
                mg_copy(g, i).wait_recv()

        @pl.loop(0, 4)
        def _(b):
            gr_acc[b] = right_terms(b, 0, early)

    stages = {
        "a": lambda g: send_a(g).start(),
        "h": make_hidden,
        "m": lambda g: make_mixed(),
        "s": lambda g: send_mixed(),
        "w": lambda g: wait_mixed(),
        "d": lambda g: load_down.wait(),
        "t": make_target,
        "c": combine,
        "g": lambda g: make_grads(g, g == 0),
        "r": lambda g: early_right(),
    }
    for step in PLAN:
        stages[step[0]](int(step[1:] or 0))

    def gl_copy(d):
        peer = lax.rem(z + d, T)
        return pltpu.make_async_remote_copy(
            gl_s.at[:, peer], gl_out.at[pl.ds(z * na, na)], gl_send.at[d], gl_recv.at[d],
            **along(peer))

    def gr_copy(b):
        return pltpu.make_async_remote_copy(
            gr_s.at[b], gr_out.at[z], gr_send.at[b], gr_recv.at[z], **along(b))

    shape = (na * nk, 4 * nf)
    keep = iota(shape, 0) // nk == lax.rem(iota(shape, 1), na)
    fold = iota((4 * nf, nb), 1) == (iota((4 * nf, nb), 0) // nf) * ni + lax.rem(
        iota((4 * nf, nb), 0), nf) // na
    total = jnp.dot(
        jnp.where(keep, gl_acc[...], 0.0).astype(bf16), fold.astype(f32).astype(bf16),
        preferred_element_type=f32)
    gl_s[...] = total.astype(bf16).reshape(na, T, nk // T, nb)
    for d in range(1, T):
        gl_copy(d).start()
    gl_out[pl.ds(z * na, na)] = gl_s[:, z]

    def finish_right(b):
        gr_s[b] = (gr_acc[b] + right_terms(b, early, parts)).astype(bf16)

        @pl.when(b != z)
        def _():
            gr_copy(b).start()

        @pl.when(b == z)
        def _():
            gr_out[z] = gr_s[b]

    finish_right(f)
    for i in (2, 0, 1):
        for g in range(LATE, G):
            mg_copy(g, i).wait_recv()
        finish_right(peers[i])

    for d in range(1, T):
        gl_copy(d).wait()
    for b in range(T):
        @pl.when(z != b)
        def _():
            gr_copy(b).wait_send()
            pltpu.make_async_remote_copy(
                gr_s.at[b], gr_out.at[b], gr_send.at[b], gr_recv.at[b], **along(b)).wait_recv()

    tok_near.wait_send()
    for i, j in pieces:
        tok_cross(i, j).wait_send()
        tok_pass(i, j).wait_send()
    for i in range(3):
        mix_copy(i).wait_send()
    for g in range(G):
        if g > 0:
            send_a(g).wait_send()
        for cp in (send_hx(g), send_hp(g), send_r(g)):
            cp.wait_send()
        z_near(g, None).wait_send()
        for k in range(2):
            @pl.when(inner)
            def _():
                z_far(g, k).wait_send()

            @pl.when(jnp.logical_not(inner))
            def _():
                z_near(g, k).wait_send()

        for i in range(3):
            mg_copy(g, i).wait_send()

    def drain(t, carry):
        for p in range(2):
            pair_copy(p, t).wait_send()
        send_first(t).wait_send()
        return carry

    lax.fori_loop(0, n, drain, 0)


def fused_body(tokens, gate_weight, up_weight, down_weight, right_factor, left_factor):
    T = lax.axis_size("tensor")
    rows = SUB
    parts = tokens.shape[0] // rows
    tok = tokens.reshape(parts, rows, tokens.shape[1])
    features, hidden = gate_weight.shape
    width = CHUNK
    n = hidden // width
    G = len(GROUPS)
    cols = down_weight.shape[1] // T
    bf16, f32 = jnp.bfloat16, jnp.float32
    dma = pltpu.SemaphoreType.DMA
    anyspace = pl.BlockSpec(memory_space=pl.ANY)
    vmem = pl.BlockSpec(memory_space=pltpu.VMEM)
    ni, nkr, nj = right_factor.shape
    na, nkl, nb = left_factor.shape[0] // T, left_factor.shape[1], left_factor.shape[2]
    nf, nk = na * ni, nkl * T
    N = 4 * parts * rows
    right_parts, left_parts = pl.pallas_call(
        functools.partial(layer_kernel, n, T, width, cols),
        out_shape=(
            jax.ShapeDtypeStruct((T, nf, nj), bf16),
            jax.ShapeDtypeStruct((T * na, nkl, nb), bf16),
        ),
        in_specs=[anyspace] * 6,
        out_specs=(vmem, vmem),
        scratch_shapes=[
            pltpu.VMEM((DEPTH, features, width), bf16),
            pltpu.VMEM((DEPTH, features, width), bf16),
            pltpu.VMEM((hidden, T * cols), bf16),
            pltpu.VMEM((2, 2, parts, 2, rows, hidden), bf16),
            pltpu.VMEM((2, parts, 2, rows, hidden), bf16),
            pltpu.VMEM((parts, 2, rows, hidden), bf16),
            pltpu.VMEM((parts, 4, rows, hidden), bf16),
            pltpu.VMEM((T, N, cols), bf16),
            pltpu.VMEM((4, N, cols), bf16),
            pltpu.VMEM((parts, 4, rows, features), bf16),
            pltpu.VMEM((ni, nkr, nj), bf16),
            pltpu.VMEM((T, nf, nj), bf16),
            pltpu.VMEM((T, nf, nj), bf16),
            pltpu.VMEM((na, T, nkl, nb), bf16),
            pltpu.VMEM((4 * nf, features), bf16),
            pltpu.VMEM((na * nk, 4 * nf), bf16),
            pltpu.VMEM((N, 4 * nf), bf16),
            pltpu.VMEM((N, 4 * nf), bf16),
            pltpu.VMEM((N, 4 * nf), bf16),
            pltpu.VMEM((4, N, nf), bf16),
            pltpu.VMEM((4, nf, nj), f32),
            pltpu.VMEM((4, nf, nj), bf16),
            pltpu.VMEM((na * nk, 4 * nf), f32),
            pltpu.VMEM((na, T, nkl, nb), bf16),
            dma((2,)), dma((2,)), dma((2, 2)), dma((2, 2)), dma((2, 2)), dma((2, 2)),
            dma((2, DEPTH)), dma,
            dma((2, n)), dma((2, n)), dma((n,)), dma((n,)), dma((G,)), dma((G,)),
            dma((G,)), dma((G,)), dma((G,)), dma((G,)), dma((G,)), dma((G,)),
            dma((G, 3)), dma((G, 4)),
            dma((T,)), dma((T,)), dma((T,)), dma((T,)),
            dma((3,)), dma((3,)), dma((G, 3)), dma((G, 3)),
            dma((T,)), dma((T,)), dma((T,)), dma((T,)),
        ],
        compiler_params=pltpu.CompilerParams(
            collective_id=0, has_side_effects=True, vmem_limit_bytes=62 * 1024 * 1024
        ),
        name="layer",
    )(tok, gate_weight, up_weight, down_weight, right_factor, left_factor)

    def widen(right_ref, left_ref, right_out, left_out):
        for t in range(T):
            right_out[:, t * na:(t + 1) * na] = right_ref[t].astype(f32).reshape(ni, na, nj)
        left_out[...] = left_ref[...].astype(f32)

    return pl.pallas_call(
        widen,
        out_shape=(
            jax.ShapeDtypeStruct((ni, nkr, nj), f32),
            jax.ShapeDtypeStruct((T * na, nkl, nb), f32),
        ),
        in_specs=[vmem] * 2,
        out_specs=(vmem, vmem),
        name="widen",
    )(right_parts, left_parts)


def body(tokens, gate_weight, up_weight, down_weight, right_factor, left_factor):
    F, T = lax.axis_size("fsdp"), lax.axis_size("tensor")
    fits = (
        F == 4
        and T == 4
        and gate_weight.shape[1] % CHUNK == 0
        and left_factor.shape[0] % T == 0
        and right_factor.shape[1] % T == 0
        and gate_weight.shape[0] <= 2048
        and tokens.shape[0] == 128
    )
    run = fused_body if fits else plain_body
    return run(tokens, gate_weight, up_weight, down_weight, right_factor, left_factor)


def solution(mesh):
    return jax.shard_map(
        body,
        mesh=mesh,
        in_specs=(
            P(("groups", "fsdp"), None),
            P("fsdp", "tensor"),
            P("fsdp", "tensor"),
            P("tensor", "fsdp"),
            P("fsdp", "tensor", None),
            P("fsdp", "tensor", None),
        ),
        out_specs=(P(("groups", "fsdp"), "tensor", None), P(("groups", "fsdp"), "tensor", None)),
        check_vma=False,
    )
```

```python
import functools
import math

import jax
import jax.numpy as jnp
from jax import lax
from jax.experimental import pallas as pl
from jax.experimental.pallas import tpu as pltpu
from jax.sharding import PartitionSpec as P

MESH = pl.DeviceIdType.MESH
CHUNK = 512
SUB = 16
GROUPS = ((0, 2), (2, 4), (4, 6), (6, 7), (7, 8))
DEPTH = 3
LATE = 2
PLAN = (
    "h0", "h1", "a2", "a3", "m", "d", "t0", "t1", "c0", "h2",
    "a4", "c1", "t2", "h3", "h4", "s", "t3", "c2", "t4", "c3",
    "w", "g0", "g1", "c4", "g2", "g3", "r", "g4",
)


def plain_body(tokens, gate_weight, up_weight, down_weight, right_factor, left_factor):
    fsdp_count = lax.axis_size("fsdp")
    tensor_count = lax.axis_size("tensor")
    tok_local = tokens.shape[0]
    group_rows = tok_local * fsdp_count
    share_rows = group_rows // tensor_count
    hid_local = gate_weight.shape[1]
    spread = lax.all_to_all(tokens, "fsdp", split_axis=1, concat_axis=0, tiled=True)
    student_in = lax.dynamic_slice_in_dim(
        spread, lax.axis_index("tensor") * share_rows, share_rows, 0
    )
    gate_part = jnp.dot(spread, gate_weight, preferred_element_type=jnp.float32)
    up_part = jnp.dot(spread, up_weight, preferred_element_type=jnp.float32)
    partial_value = jnp.concatenate([gate_part, up_part], axis=1)
    summed = lax.psum(partial_value.astype(jnp.bfloat16), "fsdp").astype(jnp.float32)
    hidden = (jax.nn.silu(summed[:, :hid_local]) * summed[:, hid_local:]).astype(jnp.bfloat16)
    target = lax.psum_scatter(
        jnp.dot(hidden, down_weight, preferred_element_type=jnp.float32).astype(jnp.bfloat16),
        "tensor",
        scatter_dimension=0,
        tiled=True,
    ).astype(jnp.float32)
    right_full, left_full = (
        lax.all_gather(right_factor, "tensor", axis=1, tiled=True),
        lax.all_gather(left_factor, "tensor", axis=1, tiled=True),
    )
    blocks_local = right_full.shape[0]
    block_size = right_full.shape[2]
    block_input = student_in.reshape(share_rows, blocks_local, block_size)
    mixed = jnp.einsum(
        "nij,ikj->nik", block_input, right_full, preferred_element_type=jnp.float32
    ).astype(jnp.bfloat16)
    routed = lax.all_to_all(mixed, "fsdp", split_axis=2, concat_axis=1, tiled=True)
    student = jnp.einsum("nij,jki->njk", routed, left_full, preferred_element_type=jnp.float32)
    inv_root = 1.0 / math.sqrt(group_rows)
    out_grad = (student - target.reshape(student.shape)) * inv_root
    grad_left = jnp.einsum("njk,nij->jki", out_grad, routed.astype(jnp.float32))
    mixed_grad = jnp.einsum("njk,jki->nij", out_grad, left_full.astype(jnp.float32)).astype(
        jnp.bfloat16
    )
    returned = lax.all_to_all(mixed_grad, "fsdp", split_axis=1, concat_axis=2, tiled=True)
    grad_right = jnp.einsum(
        "nik,nij->ikj", returned.astype(jnp.float32), block_input.astype(jnp.float32)
    )
    grad_right, grad_left = (
        lax.psum_scatter(grad_right, "tensor", scatter_dimension=1, tiled=True),
        lax.psum_scatter(grad_left, "tensor", scatter_dimension=1, tiled=True),
    )
    return (grad_right, grad_left)


def layer_kernel(
    n, T, width, cols,
    tok, gw, uw, dw, right, left, gr_out, gl_out,
    wg, wu, wd, pbuf, recv_p, recv_x, hid, t_send, t_recv,
    spread, rload, r_s, rki, lji, rbig, lbig, mix_s, routed, mg_s, mg_r, gr_acc, gr_s, gl_acc, gl_s,
    tok_send, tok_recv, tx_send, tx_recv, tf_send, tf_recv, w_sem, d_sem,
    p_send, p_recv, first_send, first_recv, a_send, a_recv, hx_send, hx_recv, hp_send, hp_recv, r_send, r_recv,
    z_send, z_recv, rf_send, rf_recv, lf_send, lf_recv, mix_send, mix_recv, mg_send, mg_recv,
    gr_send, gr_recv, gl_send, gl_recv,
):
    f32, bf16 = jnp.float32, jnp.bfloat16
    f = lax.axis_index("fsdp")
    z = lax.axis_index("tensor")
    x, c = f // 2, f % 2
    partner = x * 2 + (1 - c)
    across = (1 - x) * 2 + c
    diag = (1 - x) * 2 + (1 - c)
    peers = (across, diag, partner)
    parts, rows, features = spread.shape[0], spread.shape[2], spread.shape[3]
    N = parts * 4 * rows
    G = len(GROUPS)
    ni, nk_local, nj = right.shape
    na = nk_local // T
    nk, nb = left.shape[1] * T, left.shape[2]
    nf = na * ni
    iota = functools.partial(lax.broadcasted_iota, jnp.int32)

    def to(peer):
        return dict(device_id={"fsdp": peer}, device_id_type=MESH)

    def along(peer):
        return dict(device_id={"tensor": peer}, device_id_type=MESH)

    def tile(t):
        return pl.ds(pl.multiple_of(t * width, width), width)

    def token_rows(g):
        return slice(GROUPS[g][0] * 4 * rows, GROUPS[g][1] * 4 * rows)

    def weights(t):
        s = lax.rem(t, DEPTH)
        cc = tile(lax.rem(t, n))
        return (
            pltpu.make_async_copy(gw.at[:, cc], wg.at[s], w_sem.at[0, s]),
            pltpu.make_async_copy(uw.at[:, cc], wu.at[s], w_sem.at[1, s]),
        )

    def feature_columns(peer):
        return pl.ds(pl.multiple_of(peer * features, features), features)

    own = pltpu.make_async_copy(
        tok.at[:, :, feature_columns(f)], spread.at[:, f], tok_send.at[0])
    own.start()
    for t in range(DEPTH - 1):
        for cp in weights(t):
            cp.start()
    load_right = pltpu.make_async_copy(right, rload, rf_send.at[0])
    load_right.start()

    barrier = pltpu.get_barrier_semaphore()
    for peer in peers:
        pl.semaphore_signal(barrier, inc=1, **to(peer))
    for d in range(1, T):
        pl.semaphore_signal(barrier, inc=1, **along(lax.rem(z + d, T)))
    load_right.wait()
    wide_right = rload[...].astype(f32)
    for p in range(T):
        r_s[p] = wide_right[:, p * na:(p + 1) * na].reshape(nf, nj).astype(bf16)

    pl.semaphore_wait(barrier, 3 + T - 1)

    half = lax.rem(z, 2)
    z_mate = z + 1 - 2 * half
    span = parts // 4

    def tok_cross(i, j):
        mm = pl.ds(half * (parts // 2) + j * span, span)
        return pltpu.make_async_remote_copy(
            tok.at[mm, :, feature_columns(peers[i])], spread.at[mm, f],
            tx_send.at[i, j], tx_recv.at[i, j], **to(peers[i]))

    def tok_pass(i, j):
        mm = pl.ds(half * (parts // 2) + j * span, span)
        return pltpu.make_async_remote_copy(
            spread.at[mm, peers[i]], spread.at[mm, peers[i]],
            tf_send.at[i, j], tf_recv.at[i, j], **along(z_mate))

    tok_near = pltpu.make_async_remote_copy(
        tok.at[:, :, feature_columns(partner)], spread.at[:, f],
        tok_send.at[1], tok_recv.at[1], **to(partner))
    tok_near.start()
    pieces = [(i, j) for j in range(2) for i in range(2)]
    for i, j in pieces:
        tok_cross(i, j).start()

    def right_copy(d):
        peer = lax.rem(z + d, T)
        return pltpu.make_async_remote_copy(
            r_s.at[peer], rki.at[z], rf_send.at[d], rf_recv.at[d], **along(peer))

    def left_copy(d):
        peer = lax.rem(z + d, T)
        return pltpu.make_async_remote_copy(
            left.at[pl.ds(peer * na, na)], lji.at[:, z], lf_send.at[d], lf_recv.at[d],
            **along(peer))

    factors = [right_copy(d) for d in range(1, T)] + [left_copy(d) for d in range(1, T)]
    for cp in factors:
        cp.start()
    own_left = pltpu.make_async_copy(left.at[pl.ds(z * na, na)], lji.at[:, z], lf_send.at[0])
    own_left.start()
    rki[z] = r_s[z]

    def pair_copy(p, t):
        cc = tile(t)
        return pltpu.make_async_remote_copy(
            pbuf.at[p, 1 - c, :, :, :, cc], recv_p.at[p, :, :, :, cc],
            p_send.at[p, t], p_recv.at[p, t], **to(partner))

    def send_first(t):
        mm = slice(*GROUPS[0])
        cc = tile(t)
        return pltpu.make_async_remote_copy(
            pbuf.at[0, c, mm, :, :, cc], recv_x.at[mm, :, :, cc],
            first_send.at[t], first_recv.at[t], **to(across))

    def pair_sum(p, t):
        pair_copy(p, t).wait_recv()
        cc = tile(t)
        for k in range(2):
            total = pbuf[p, c, :, k, :, cc].astype(f32) + recv_p[p, :, k, :, cc].astype(f32)
            pbuf[p, c, :, k, :, cc] = total.astype(bf16)
        if p == 0:
            send_first(t).start()

    def products(p, t):
        chip = x if p == 0 else 1 - x
        step = p * n + t

        @pl.when(step + DEPTH - 1 < 2 * n)
        def _():
            for cp in weights(step + DEPTH - 1):
                cp.start()

        for cp in weights(step):
            cp.wait()
        s = lax.rem(step, DEPTH)
        toks = spread[:, pl.ds(2 * chip, 2)].reshape(parts * 2 * rows, features)
        cc = tile(t)
        for k, w in ((0, wg), (1, wu)):
            part = jnp.dot(toks, w[s], preferred_element_type=f32).astype(bf16)
            part = part.reshape(parts, 2, rows, width)
            for h in range(2):
                pbuf[p, h, :, k, :, cc] = part[:, h]
        pair_copy(p, t).start()

        @pl.when(t >= 1)
        def _():
            pair_sum(p, t - 1)

    own.wait()
    tok_near.wait_recv()

    def first_half(t, carry):
        products(0, t)
        for q, (i, j) in enumerate(pieces):
            @pl.when(t == 2 * q + 1)
            def _():
                tok_cross(i, j).wait_recv()
                tok_pass(i, j).start()
        return carry

    lax.fori_loop(0, n, first_half, 0)
    pair_sum(0, n - 1)

    def send_a(g):
        mm = slice(*GROUPS[g])
        return pltpu.make_async_remote_copy(
            pbuf.at[0, c, mm], recv_x.at[mm], a_send.at[g], a_recv.at[g], **to(across))

    send_a(1).start()
    for q, (i, j) in enumerate(pieces):
        if 2 * q + 1 >= n:
            tok_cross(i, j).wait_recv()
            tok_pass(i, j).start()

    own_left.wait()
    for cp in factors:
        cp.wait()
    packed = rki[...].reshape(T * nf, nj)
    lane_block = lax.rem(iota((T * nf, nj), 0), nf) // na
    for i in range(ni):
        rbig[:, i * nj:(i + 1) * nj] = jnp.where(lane_block == i, packed, jnp.zeros_like(packed))
    col = lax.rem(iota((nb, 4 * nf), 1), nf)
    pick = iota((nb, 4 * nf), 0) == (iota((nb, 4 * nf), 1) // nf) * ni + col // na
    wide = jnp.dot(
        lji[...].reshape(na * nk, nb), pick.astype(f32).astype(bf16), preferred_element_type=f32)
    same = iota((na * nk, 4 * nf), 0) // nk == lax.rem(iota((na * nk, 4 * nf), 1), na)
    lbig[...] = jnp.where(same, wide, 0.0).astype(bf16)

    for i, j in pieces:
        tok_pass(i, j).wait_recv()

    def second_half(t, carry):
        products(1, t)
        return carry

    lax.fori_loop(0, n, second_half, 0)
    load_down = pltpu.make_async_copy(dw, wd, d_sem)
    load_down.start()
    pair_sum(1, n - 1)

    mine = pl.ds(pl.multiple_of(f * nf, nf), nf)

    def mix_copy(i):
        return pltpu.make_async_remote_copy(
            mix_s.at[:, pl.ds(pl.multiple_of(peers[i] * nf, nf), nf)],
            routed.at[:, pl.ds(pl.multiple_of(f * nf, nf), nf)],
            mix_send.at[i], mix_recv.at[i], **to(peers[i]))

    def send_hx(g):
        mm = slice(*GROUPS[g])
        return pltpu.make_async_remote_copy(
            hid.at[mm, across], hid.at[mm, across], hx_send.at[g], hx_recv.at[g], **to(across))

    def send_hp(g):
        mm = slice(*GROUPS[g])
        return pltpu.make_async_remote_copy(
            hid.at[mm, across], hid.at[mm, across], hp_send.at[g], hp_recv.at[g], **to(partner))

    def send_r(g):
        mm = slice(*GROUPS[g])
        return pltpu.make_async_remote_copy(
            hid.at[mm, f], hid.at[mm, f], r_send.at[g], r_recv.at[g], **to(partner))

    side = z // 2
    far = 2 * (1 - side)
    inner = (z == 1) | (z == 2)

    def z_near(g, i):
        rr = token_rows(g)
        b = z_mate if i is None else far + i
        k = 0 if i is None else 1 + i
        return pltpu.make_async_remote_copy(
            t_send.at[b, rr], t_recv.at[k, rr], z_send.at[g, k], z_recv.at[g, k],
            **along(z_mate))

    def z_far(g, i):
        rr = token_rows(g)
        return pltpu.make_async_remote_copy(
            t_send.at[far + i, rr], t_recv.at[3, rr], z_send.at[g, 1 + i], z_recv.at[g, 3],
            **along(far + i))

    def mg_copy(g, i):
        rr = token_rows(g)
        return pltpu.make_async_remote_copy(
            mg_s.at[rr, pl.ds(pl.multiple_of(peers[i] * nf, nf), nf)], mg_r.at[f, rr],
            mg_send.at[g, i], mg_recv.at[g, i], **to(peers[i]))

    def make_hidden(g):
        mm = slice(*GROUPS[g])
        if g > 0:
            send_a(g).wait_recv()

        @pl.loop(0, n)
        def _(t):
            if g == 0:
                send_first(t).wait_recv()
            cc = tile(t)
            gate = pbuf[1, c, mm, 0, :, cc].astype(f32) + recv_x[mm, 0, :, cc].astype(f32)
            up = pbuf[1, c, mm, 1, :, cc].astype(f32) + recv_x[mm, 1, :, cc].astype(f32)
            hid[mm, across, :, cc] = (jax.nn.silu(gate) * up).astype(bf16)

        send_hx(g).start()
        send_hp(g).start()

    def make_target(g):
        m0, m1 = GROUPS[g]
        rr = token_rows(g)
        send_hx(g).wait_recv()
        send_r(g).start()
        send_hp(g).wait_recv()
        send_r(g).wait_recv()

        @pl.loop(0, T)
        def _(i):
            b = 2 * lax.rem(side + 1 + i // 2, 2) + lax.rem(i + (i // 2) * (z + 1), 2)
            cc = pl.ds(pl.multiple_of(b * cols, cols), cols)
            h = hid[m0:m1].reshape((m1 - m0) * 4 * rows, n * width)
            t_send[b, rr] = jnp.dot(h, wd[:, cc], preferred_element_type=f32).astype(bf16)

            for k in range(2):
                @pl.when((i == k) & jnp.logical_not(inner))
                def _():
                    z_near(g, k).start()

            @pl.when(i == 2)
            def _():
                z_near(g, None).start()

    def combine(g):
        rr = token_rows(g)

        @pl.when(inner)
        def _():
            for k in range(2):
                z_near(g, k).wait_recv()
                total = t_send[far + k, rr].astype(f32) + t_recv[1 + k, rr].astype(f32)
                t_send[far + k, rr] = total.astype(bf16)
                z_far(g, k).start()

    def make_grads(g, first):
        rr = token_rows(g)
        student = lax.dot_general(
            routed[rr], lbig[...], (((1,), (1,)), ((), ())), preferred_element_type=f32)
        z_near(g, None).wait_recv()
        z_far(g, 0).wait_recv()
        tgt = t_send[z, rr].astype(f32) + t_recv[0, rr].astype(f32) + t_recv[3, rr].astype(f32)
        out_grad = (student - tgt) * (1.0 / math.sqrt(N))
        mg_s[rr] = jnp.dot(
            out_grad.astype(bf16), lbig[...], preferred_element_type=f32).astype(bf16)
        for i in range(3):
            mg_copy(g, i).start()
        mg_r[f, rr] = mg_s[rr, mine]
        part = jnp.dot(out_grad.T.astype(bf16), routed[rr], preferred_element_type=f32)
        if first:
            gl_acc[...] = part
        else:
            gl_acc[...] += part

    row_block = iota((nf, nj), 0) // na

    def right_terms(b, m0, m1):
        rr = slice(m0 * 4 * rows, m1 * 4 * rows)
        flipped = mg_r[b, rr].astype(f32).T.astype(bf16)
        total = jnp.zeros((nf, nj), f32)
        for i in range(0, ni, 2):
            rhs = spread[m0:m1, :, :, i * nj:(i + 2) * nj].reshape((m1 - m0) * 4 * rows, 2 * nj)
            part = jnp.dot(flipped, rhs, preferred_element_type=f32)
            for k in range(2):
                total += jnp.where(row_block == i + k, part[:, k * nj:(k + 1) * nj], 0.0)
        return total

    def make_mixed():
        mix_s[...] = lax.dot_general(
            spread[...].reshape(N, features), rbig[...], (((1,), (1,)), ((), ())),
            preferred_element_type=f32).astype(bf16)
        routed[:, mine] = mix_s[:, mine]

    def send_mixed():
        for i in range(3):
            mix_copy(i).start()

    def wait_mixed():
        for i in range(3):
            mix_copy(i).wait_recv()

    early = GROUPS[LATE][0]

    def early_right():
        for g in range(LATE):
            for i in range(3):
                mg_copy(g, i).wait_recv()

        @pl.loop(0, 4)
        def _(b):
            gr_acc[b] = right_terms(b, 0, early)

    stages = {
        "a": lambda g: send_a(g).start(),
        "h": make_hidden,
        "m": lambda g: make_mixed(),
        "s": lambda g: send_mixed(),
        "w": lambda g: wait_mixed(),
        "d": lambda g: load_down.wait(),
        "t": make_target,
        "c": combine,
        "g": lambda g: make_grads(g, g == 0),
        "r": lambda g: early_right(),
    }
    for step in PLAN:
        stages[step[0]](int(step[1:] or 0))

    def gl_copy(d):
        peer = lax.rem(z + d, T)
        return pltpu.make_async_remote_copy(
            gl_s.at[:, peer], gl_out.at[pl.ds(z * na, na)], gl_send.at[d], gl_recv.at[d],
            **along(peer))

    def gr_copy(b):
        return pltpu.make_async_remote_copy(
            gr_s.at[b], gr_out.at[z], gr_send.at[b], gr_recv.at[z], **along(b))

    shape = (na * nk, 4 * nf)
    keep = iota(shape, 0) // nk == lax.rem(iota(shape, 1), na)
    fold = iota((4 * nf, nb), 1) == (iota((4 * nf, nb), 0) // nf) * ni + lax.rem(
        iota((4 * nf, nb), 0), nf) // na
    total = jnp.dot(
        jnp.where(keep, gl_acc[...], 0.0).astype(bf16), fold.astype(f32).astype(bf16),
        preferred_element_type=f32)
    gl_s[...] = total.astype(bf16).reshape(na, T, nk // T, nb)
    for d in range(1, T):
        gl_copy(d).start()
    gl_out[pl.ds(z * na, na)] = gl_s[:, z]

    def finish_right(b):
        gr_s[b] = (gr_acc[b] + right_terms(b, early, parts)).astype(bf16)

        @pl.when(b != z)
        def _():
            gr_copy(b).start()

        @pl.when(b == z)
        def _():
            gr_out[z] = gr_s[b]

    finish_right(f)
    for i in (2, 0, 1):
        for g in range(LATE, G):
            mg_copy(g, i).wait_recv()
        finish_right(peers[i])

    for d in range(1, T):
        gl_copy(d).wait()
    for b in range(T):
        @pl.when(z != b)
        def _():
            gr_copy(b).wait_send()
            pltpu.make_async_remote_copy(
                gr_s.at[b], gr_out.at[b], gr_send.at[b], gr_recv.at[b], **along(b)).wait_recv()

    tok_near.wait_send()
    for i, j in pieces:
        tok_cross(i, j).wait_send()
        tok_pass(i, j).wait_send()
    for i in range(3):
        mix_copy(i).wait_send()
    for g in range(G):
        if g > 0:
            send_a(g).wait_send()
        for cp in (send_hx(g), send_hp(g), send_r(g)):
            cp.wait_send()
        z_near(g, None).wait_send()
        for k in range(2):
            @pl.when(inner)
            def _():
                z_far(g, k).wait_send()

            @pl.when(jnp.logical_not(inner))
            def _():
                z_near(g, k).wait_send()

        for i in range(3):
            mg_copy(g, i).wait_send()

    def drain(t, carry):
        for p in range(2):
            pair_copy(p, t).wait_send()
        send_first(t).wait_send()
        return carry

    lax.fori_loop(0, n, drain, 0)


def fused_body(tokens, gate_weight, up_weight, down_weight, right_factor, left_factor):
    T = lax.axis_size("tensor")
    rows = SUB
    parts = tokens.shape[0] // rows
    tok = tokens.reshape(parts, rows, tokens.shape[1])
    features, hidden = gate_weight.shape
    width = CHUNK
    n = hidden // width
    G = len(GROUPS)
    cols = down_weight.shape[1] // T
    bf16, f32 = jnp.bfloat16, jnp.float32
    dma = pltpu.SemaphoreType.DMA
    anyspace = pl.BlockSpec(memory_space=pl.ANY)
    vmem = pl.BlockSpec(memory_space=pltpu.VMEM)
    ni, nkr, nj = right_factor.shape
    na, nkl, nb = left_factor.shape[0] // T, left_factor.shape[1], left_factor.shape[2]
    nf, nk = na * ni, nkl * T
    N = 4 * parts * rows
    right_parts, left_parts = pl.pallas_call(
        functools.partial(layer_kernel, n, T, width, cols),
        out_shape=(
            jax.ShapeDtypeStruct((T, nf, nj), bf16),
            jax.ShapeDtypeStruct((T * na, nkl, nb), bf16),
        ),
        in_specs=[anyspace] * 6,
        out_specs=(vmem, vmem),
        scratch_shapes=[
            pltpu.VMEM((DEPTH, features, width), bf16),
            pltpu.VMEM((DEPTH, features, width), bf16),
            pltpu.VMEM((hidden, T * cols), bf16),
            pltpu.VMEM((2, 2, parts, 2, rows, hidden), bf16),
            pltpu.VMEM((2, parts, 2, rows, hidden), bf16),
            pltpu.VMEM((parts, 2, rows, hidden), bf16),
            pltpu.VMEM((parts, 4, rows, hidden), bf16),
            pltpu.VMEM((T, N, cols), bf16),
            pltpu.VMEM((4, N, cols), bf16),
            pltpu.VMEM((parts, 4, rows, features), bf16),
            pltpu.VMEM((ni, nkr, nj), bf16),
            pltpu.VMEM((T, nf, nj), bf16),
            pltpu.VMEM((T, nf, nj), bf16),
            pltpu.VMEM((na, T, nkl, nb), bf16),
            pltpu.VMEM((4 * nf, features), bf16),
            pltpu.VMEM((na * nk, 4 * nf), bf16),
            pltpu.VMEM((N, 4 * nf), bf16),
            pltpu.VMEM((N, 4 * nf), bf16),
            pltpu.VMEM((N, 4 * nf), bf16),
            pltpu.VMEM((4, N, nf), bf16),
            pltpu.VMEM((4, nf, nj), f32),
            pltpu.VMEM((4, nf, nj), bf16),
            pltpu.VMEM((na * nk, 4 * nf), f32),
            pltpu.VMEM((na, T, nkl, nb), bf16),
            dma((2,)), dma((2,)), dma((2, 2)), dma((2, 2)), dma((2, 2)), dma((2, 2)),
            dma((2, DEPTH)), dma,
            dma((2, n)), dma((2, n)), dma((n,)), dma((n,)), dma((G,)), dma((G,)),
            dma((G,)), dma((G,)), dma((G,)), dma((G,)), dma((G,)), dma((G,)),
            dma((G, 3)), dma((G, 4)),
            dma((T,)), dma((T,)), dma((T,)), dma((T,)),
            dma((3,)), dma((3,)), dma((G, 3)), dma((G, 3)),
            dma((T,)), dma((T,)), dma((T,)), dma((T,)),
        ],
        compiler_params=pltpu.CompilerParams(
            collective_id=0, has_side_effects=True, vmem_limit_bytes=62 * 1024 * 1024
        ),
        name="layer",
    )(tok, gate_weight, up_weight, down_weight, right_factor, left_factor)

    def widen(right_ref, left_ref, right_out, left_out):
        for t in range(T):
            right_out[:, t * na:(t + 1) * na] = right_ref[t].astype(f32).reshape(ni, na, nj)
        left_out[...] = left_ref[...].astype(f32)

    return pl.pallas_call(
        widen,
        out_shape=(
            jax.ShapeDtypeStruct((ni, nkr, nj), f32),
            jax.ShapeDtypeStruct((T * na, nkl, nb), f32),
        ),
        in_specs=[vmem] * 2,
        out_specs=(vmem, vmem),
        name="widen",
    )(right_parts, left_parts)


def body(tokens, gate_weight, up_weight, down_weight, right_factor, left_factor):
    F, T = lax.axis_size("fsdp"), lax.axis_size("tensor")
    fits = (
        F == 4
        and T == 4
        and gate_weight.shape[1] % CHUNK == 0
        and left_factor.shape[0] % T == 0
        and right_factor.shape[1] % T == 0
        and gate_weight.shape[0] <= 2048
        and tokens.shape[0] == 128
    )
    run = fused_body if fits else plain_body
    return run(tokens, gate_weight, up_weight, down_weight, right_factor, left_factor)


def solution(mesh):
    return jax.shard_map(
        body,
        mesh=mesh,
        in_specs=(
            P(("groups", "fsdp"), None),
            P("fsdp", "tensor"),
            P("fsdp", "tensor"),
            P("tensor", "fsdp"),
            P("fsdp", "tensor", None),
            P("fsdp", "tensor", None),
        ),
        out_specs=(P(("groups", "fsdp"), "tensor", None), P(("groups", "fsdp"), "tensor", None)),
        check_vma=False,
    )
```
